32 devices in a mesh: parts: 2 (over x), tile: 16 (over z, y, core).
Axes of the slice: x: 2, y: 2, z: 4, core: 2. Of those that a mesh axis runs over, the one named last changes fastest.
Arguments:
- images: bfloat16 [8, 4096, 256], P('parts', 'tile'), parts along dimension 0, may hold values from -6 to 6
- section_order: int32 [6], P('parts'), parts along dimension 0, may hold values from 0 to 2, each once
- prev_field: float32 [4, 2048, 128], P('parts', 'tile'), parts along dimension 0, may hold values from -8 to 8
- conv1_weight: bfloat16 [32, 9], replicated, may hold values from -2 to 2
- conv1_bias: float32 [32], replicated, may hold values from -3 to 3
- conv2_weight: bfloat16 [9, 32, 32], replicated, may hold values from -0.375 to 0.375
- conv2_bias: float32 [32], replicated, may hold values from -3 to 3
Outputs:
- fields: float32 [6, 2, 2048, 128], P('parts', None, 'tile'), parts along dimension 0
The draws below stay inside these ranges and needn't reach their ends.
There are 2 independent parts, one for each index of `parts`. The reference program is written for one: setup_inputs(seed, part) draws one part's arguments, and reference() takes and returns one part's arrays. A program takes and returns all parts, laid end to end along the dimension named above; an argument that names none is the same for every part. Nothing has to cross between parts.
Inputs may be any that keep to these rules, and one draw needn't show every extreme that they name: section_order is a permutation of 0 .. 2.
All inputs are finite; a program needn't handle non-finite values.
Results may differ from the reference program's by a relative error of at most 0.0043.
Values may be sent and summed in bfloat16 or wider, within the bound.
No kernel may reach another device: no remote copies, remote signals or barrier semaphores. Data moves between devices by JAX's collectives and lax.ppermute only.
A program may use at most 64 MiB of HBM per device.

```python
import jax
import jax.numpy as jnp
import numpy as np
from jax import lax

CH = 32
TILE = 256
SECT = 3
FH = 128
ROWS = 4096
FROWS = 2048


def block_levels(key, dims, split, low, high):
    gain, own = 1.0, jax.random.fold_in(key, 6)
    for axis_at, parts in split:
        steps = jnp.exp(jax.random.uniform(jax.random.fold_in(own, axis_at), (parts,), jnp.float32, low / len(split), high / len(split)))
        gain = gain * jnp.repeat(steps, dims[axis_at] // parts).reshape([-1 if axis == axis_at else 1 for axis in range(len(dims))])
    return gain


def noise(rng, extent, deviation, most, cuts=(), kind=jnp.bfloat16):
    drawn = deviation * jax.random.normal(rng, extent, jnp.float32)
    if cuts:
        drawn = drawn * block_levels(rng, extent, cuts, -0.22, 0.18)
    return jnp.clip(drawn, -most, most).astype(kind)


def setup_inputs(seed: int = 0, part: int = 0) -> dict:
    splits = jax.random.split(jax.random.key(seed), 8)
    part_keys = jax.random.split(jax.random.fold_in(splits[7], part), 8)
    return {
        "images": noise(part_keys[0], (SECT + 1, ROWS, TILE), 1.0, 6.0, ((1, 16),)),
        "section_order": jax.random.permutation(part_keys[1], SECT).astype(jnp.int32),
        "prev_field": noise(part_keys[2], (2, FROWS, FH), 2.0, 8.0, ((1, 16),), jnp.float32),
        "conv1_weight": noise(splits[3], (CH, 9), 9 ** -0.5, 2.0),
        "conv1_bias": noise(splits[4], (CH,), 0.5, 3.0, (), jnp.float32),
        "conv2_weight": noise(splits[5], (9, CH, CH), (9 * CH) ** -0.5, 0.375),
        "conv2_bias": noise(splits[6], (CH,), 0.5, 3.0, (), jnp.float32),
    }


sharpness_divisor = 16.0


def tent_weight(offset_value):
    return jnp.maximum(0.0, 1.0 - jnp.abs(offset_value))


def offset_table():
    pairs = [[row_step, col_step] for row_step in range(-4, 5) for col_step in range(-4, 5)]
    return jnp.asarray(np.array(pairs, dtype=np.int32))


def encode_section(section_image, conv1_weight, conv1_bias, conv2_weight, conv2_bias):
    planes = section_image.astype(jnp.float32)[None, None]
    depth_number = conv1_weight.shape[0]
    kernel_one = conv1_weight.astype(jnp.float32).reshape(depth_number, 1, 3, 3)
    first_out = lax.conv_general_dilated(planes, kernel_one, (2, 2), ((1, 1), (1, 1)), precision=lax.Precision.HIGHEST)[0]
    first_out = jnp.maximum(first_out + conv1_bias[:, None, None], 0.0).astype(jnp.bfloat16)
    kernel_two = conv2_weight.astype(jnp.float32).reshape(3, 3, depth_number, depth_number).transpose(2, 3, 0, 1)
    second = lax.conv_general_dilated(first_out.astype(jnp.float32)[None], kernel_two, (1, 1), ((1, 1), (1, 1)), precision=lax.Precision.HIGHEST)[0]
    return jnp.tanh(second + conv2_bias[:, None, None])


def correlate(current_features, previous):
    depth_number, row_count, col_count = current_features.shape
    padded = jnp.pad(previous, ((0, 0), (4, 4), (4, 4)))
    zero_plane = jnp.zeros((row_count, col_count), current_features.dtype)

    def offset_step(carry, pair):
        normalizer_total, along_rows, along_cols = carry
        start_zero = jnp.zeros((), jnp.int32)
        shifted = lax.dynamic_slice(padded, (start_zero, (pair[0] + 4).astype(jnp.int32), (pair[1] + 4).astype(jnp.int32)), (depth_number, row_count, col_count))
        similarity = (sharpness_divisor / depth_number) * jnp.sum(current_features * shifted, axis=0)
        exp_score = jnp.exp(similarity)
        return (normalizer_total + exp_score, along_rows + pair[0].astype(exp_score.dtype) * exp_score, along_cols + pair[1].astype(exp_score.dtype) * exp_score), None

    (normalizer_total, along_rows, along_cols), unused = lax.scan(offset_step, (zero_plane, zero_plane, zero_plane), offset_table())
    return jnp.stack([along_rows / normalizer_total, along_cols / normalizer_total], axis=0)


def resample(field_now, displacement):
    comps, row_count, col_count = field_now.shape
    padded = jnp.pad(field_now, ((0, 0), (4, 4), (4, 4)))

    def offset_step(total, pair):
        start_zero = jnp.zeros((), jnp.int32)
        shifted = lax.dynamic_slice(padded, (start_zero, (pair[0] + 4).astype(jnp.int32), (pair[1] + 4).astype(jnp.int32)), (comps, row_count, col_count))
        weight = tent_weight(displacement[0] - pair[0].astype(displacement.dtype)) * tent_weight(displacement[1] - pair[1].astype(displacement.dtype))
        return total + weight * shifted, None

    result, unused = lax.scan(offset_step, jnp.zeros(field_now.shape, field_now.dtype), offset_table())
    return result


def reference(images, section_order, prev_field, conv1_weight, conv1_bias, conv2_weight, conv2_bias):
    chain_order = section_order.astype(jnp.int32) + 1
    first_features = encode_section(images[0], conv1_weight, conv1_bias, conv2_weight, conv2_bias)

    def section_step(carry, section_number):
        previous, field_now = carry
        section_image = lax.dynamic_index_in_dim(images, section_number.astype(jnp.int32), 0, keepdims=False)
        current_features = encode_section(section_image, conv1_weight, conv1_bias, conv2_weight, conv2_bias)
        displacement = correlate(current_features, previous)
        composed = displacement + resample(field_now, displacement)
        return (current_features, composed), composed

    carry_start = (first_features, prev_field.astype(first_features.dtype))
    finished, results = lax.scan(section_step, carry_start, chain_order)
    return results
```

```python
import functools
import math

import jax
import jax.numpy as jnp
import numpy as np
from jax import lax
from jax.experimental import pallas as pl
from jax.experimental.pallas import tpu as pltpu
from jax.sharding import PartitionSpec as P

SHARPNESS = 16.0
REACH = 4
LANES = 128
WIDE = 256
HALO = 32
FIELD_HALO = 16
PITCH = 40
BIAS_LANE = 248
PAD = 8
WINDOWS = 8


def first_layer_selector():
    table = np.zeros((WINDOWS, WIDE, 8 * 9 + 3), np.float32)
    for window in range(WINDOWS):
        for row in range(2):
            for pixel in range(4):
                for row_tap in range(3):
                    for col_tap in range(3):
                        pixel_row = 2 * row + row_tap
                        column = 4 * window + 2 * pixel + col_tap
                        lane = PITCH * pixel_row if pixel_row < 3 else LANES + PITCH * (pixel_row - 3)
                        table[window, lane + column, 9 * (4 * row + pixel) + 3 * row_tap + col_tap] = 1
        for piece in range(3):
            table[window, BIAS_LANE + piece, 72 + piece] = 1
    return table.reshape(WINDOWS * WIDE, -1)


def second_layer_selector():
    table = np.zeros((8, 8, 9), np.float32)
    for row_in in range(2):
        for pixel_in in range(4):
            for slot, row_out in enumerate((2, -1, 0, 1)):
                for pixel_out in range(2):
                    row_step, col_step = row_in - row_out, pixel_in - 1 - pixel_out
                    if abs(row_step) <= 1 and abs(col_step) <= 1:
                        table[4 * row_in + pixel_in, 2 * slot + pixel_out, 3 * (row_step + 1) + col_step + 1] = 1
    return table


def lane_index(shape):
    return lax.broadcasted_iota(jnp.int32, shape, len(shape) - 1)


def kernel(
    sections, rows, total_rows, channels,
    meta_ref, img_ref, lo_ref, hi_ref, fld_ref, flo_ref, fhi_ref, w1_ref, w2_ref, b2_ref,
    out_ref, z_ref, x_ref, a_ref, o_ref, t_ref, f_ref,
):
    groups = a_ref.shape[0]
    span = x_ref.shape[0] // groups
    per = LANES // channels
    lane = lane_index((1, LANES))
    slot = lane // channels
    tile = meta_ref[0]
    pairs_total = total_rows // 2

    z_ref[...] = jnp.zeros_like(z_ref)
    f_ref[0, :, 0:FIELD_HALO, :] = flo_ref[...]
    f_ref[0, :, FIELD_HALO : FIELD_HALO + rows, :] = fld_ref[...]
    f_ref[0, :, FIELD_HALO + rows : 2 * FIELD_HALO + rows, :] = fhi_ref[...]

    def encode(k, carry):
        extra = REACH * (sections - k)
        section = jnp.where(k == 0, 0, 1 + meta_ref[jnp.maximum(k, 1)])
        base = pl.multiple_of(2 * extra, 8)
        for half in range(2):
            cols = slice(LANES * half, LANES * (half + 1))
            z_ref[half, pl.ds(base, HALO), :] = lo_ref[section, :, cols].astype(jnp.float32)
            z_ref[half, pl.ds(base + HALO, 2 * rows), :] = img_ref[section, :, cols].astype(jnp.float32)
            z_ref[half, pl.ds(base + HALO + 2 * rows, HALO), :] = hi_ref[section, :, cols].astype(jnp.float32)
        pair = lax.broadcasted_iota(jnp.int32, (span, LANES), 0) + tile * (rows // 2) - 1 - extra // 2
        valid = jnp.where((pair >= 0) & (pair < pairs_total), 1.0, 0.0)

        for group in range(groups):
            side, place = divmod(group, groups // 2)
            pieces = []
            for row in range(5):
                here = z_ref[side, pl.ds(HALO - 5 + row, span, stride=4), :]
                if place == 0 or (place == groups // 2 - 1 and side == 0):
                    if side == 0 and place == 0:
                        here = jnp.where(lane < LANES // 2, here, 0.0)
                    else:
                        other = z_ref[1 - side, pl.ds(HALO - 5 + row, span, stride=4), :]
                        low, high = (here, other) if side == 1 else (other, here)
                        here = jnp.where(lane < LANES // 2, low, high)
                start = PITCH * (row % 3)
                shift = (start - (2 * LANES // groups * place - 3)) % LANES
                pieces.append(pltpu.roll(here, shift, 1))
            left = jnp.where(lane < PITCH, pieces[0], jnp.where(lane < 2 * PITCH, pieces[1], pieces[2]))
            right = jnp.where(lane < PITCH, pieces[3], jnp.where(lane < BIAS_LANE - LANES, pieces[4], valid))
            x_ref[pl.ds(span * group, span), 0:LANES] = (left * valid).astype(jnp.bfloat16)
            x_ref[pl.ds(span * group, span), LANES:WIDE] = (right * valid).astype(jnp.bfloat16)

        def column(xh, carry):
            for part in range(2):
                window = xh + 4 * part
                first = jnp.dot(x_ref[...], w1_ref[window], preferred_element_type=jnp.float32)
                first = jnp.maximum(first, 0.0).reshape(groups, span, WIDE)
                edge = (lane_index((1, 1, WIDE)) // channels) % 4
                group_at = lax.broadcasted_iota(jnp.int32, (groups, 1, WIDE), 0)
                if part == 0:
                    drop = (edge == 0) & (group_at == 0) & (xh == 0)
                else:
                    drop = (edge == 3) & (group_at == groups - 1) & (xh == 3)
                first = jnp.where(drop, 0.0, first)
                first = first.reshape(groups * span, WIDE).astype(jnp.bfloat16)
                second = jnp.dot(first, w2_ref[...], preferred_element_type=jnp.float32)
                second = second.reshape(groups, span, WIDE)
                a_ref[:, PAD : PAD + span, :] = second[:, :, 0:LANES]
                for group in range(groups):
                    above = a_ref[group, PAD - 1 : PAD - 1 + span, :]
                    below = a_ref[group, PAD + 1 : PAD + 1 + span, :]
                    summed = second[group, :, LANES:WIDE] + jnp.where(lane < LANES // 2, above, below)
                    o_ref[part, group] = jnp.tanh(summed + b2_ref[...]) * valid
            for side in range(2):
                for half in range(2):
                    at = 4 * side + 2 * half
                    s0, s1, s2, s3 = o_ref[0, at], o_ref[1, at], o_ref[0, at + 1], o_ref[1, at + 1]
                    low = lane < LANES // 2
                    even = slot % 2 == 0
                    a0, a2 = jnp.where(low, s0, pltpu.roll(s2, 64, 1)), jnp.where(low, pltpu.roll(s0, 64, 1), s2)
                    a1, a3 = jnp.where(low, s1, pltpu.roll(s3, 64, 1)), jnp.where(low, pltpu.roll(s1, 64, 1), s3)
                    back = LANES - channels
                    c0, c1 = jnp.where(even, a0, pltpu.roll(a1, channels, 1)), jnp.where(even, pltpu.roll(a0, back, 1), a1)
                    c2, c3 = jnp.where(even, a2, pltpu.roll(a3, channels, 1)), jnp.where(even, pltpu.roll(a2, back, 1), a3)
                    for parity, pixel, value in ((0, 0, c0), (0, 1, c1), (1, 0, c2), (1, 1, c3)):
                        t_ref[k, 4 + 2 * xh + pixel, parity, side, half, PAD : PAD + span, :] = value
            return carry

        lax.fori_loop(0, 4, column, 0)

        def surround(at, carry):
            x_low, parity = at // 2, at % 2
            rows_at = slice(PAD, PAD + span)
            order = [(0, 0), (0, 1), (1, 0), (1, 1)]
            left = [pltpu.roll(t_ref[k, 8 + x_low, parity, s, h, rows_at, :], channels, 1) for s, h in order]
            right = [pltpu.roll(t_ref[k, 4 + x_low, parity, s, h, rows_at, :], LANES - channels, 1) for s, h in order]
            for n, (s, h) in enumerate(order):
                before = left[n - 1] if n else jnp.zeros_like(left[0])
                after = right[n + 1] if n < 3 else jnp.zeros_like(right[0])
                t_ref[k, x_low, parity, s, h, rows_at, :] = jnp.where(slot == 0, before, left[n])
                t_ref[k, 12 + x_low, parity, s, h, rows_at, :] = jnp.where(slot == per - 1, after, right[n])
            return carry

        @pl.when(k < sections)
        def _():
            lax.fori_loop(0, 8, surround, 0)

        return carry

    lax.fori_loop(0, sections + 1, encode, 0)

    scale = SHARPNESS / channels * math.log2(math.e)
    sub8 = lax.broadcasted_iota(jnp.int32, (8, LANES), 0)
    lane8 = lane_index((8, LANES))
    wide = lane_index((1, WIDE))
    x_of = (wide // 8) % 4
    y_of = 2 * (wide % 4) + (wide // 4) % 2
    row_at = 2 * lax.broadcasted_iota(jnp.int32, (2, 8, WIDE), 1) + lax.broadcasted_iota(jnp.int32, (2, 8, WIDE), 0)
    row_weight = row_at.astype(jnp.float32)
    row_mask = jnp.where((row_at >= y_of) & (row_at <= y_of + 2 * REACH), 1.0, 0.0)
    pick = channels * ((lane8 // 8) % 4) + 8 * (lane8 % 4) + 4 * (sub8 % 2) + sub8 // 2
    patch = [jnp.where(slot == q, 1.0, 0.0).astype(jnp.bfloat16) for q in range(per)]

    def gather(values, index):
        return jnp.take_along_axis(values, index, axis=1, mode="promise_in_bounds")

    def block(k, i):
        extra = REACH * (sections - k)
        down = jnp.zeros((8, LANES), jnp.float32)
        across = jnp.zeros((8, LANES), jnp.float32)
        for side in range(2):
            for h in range(2):
                lhs, rhs = [], []
                for half in range(2):
                    window = t_ref[k - 1, 4 * h : 4 * h + 12, :, side, half, pl.ds(PAD + 1 + 4 * i, 8), :]
                    lhs.append(window.reshape(12 * 16, LANES).astype(jnp.bfloat16))
                    even = t_ref[k, 4 + 4 * h : 8 + 4 * h, 0, side, half, pl.ds(PAD + 1 + 4 * i, 8), :]
                    odd = t_ref[k, 4 + 4 * h : 8 + 4 * h, 1, side, half, pl.ds(PAD - 3 + 4 * i, 8), :]
                    current = jnp.where(sub8 < 4, even, odd) * scale
                    current = current.reshape(32, LANES).astype(jnp.bfloat16)
                    nothing = jnp.zeros_like(current)
                    for q in range(per):
                        masked = current * patch[q]
                        rhs.append(jnp.concatenate([masked, nothing] if half == 0 else [nothing, masked], axis=1))
                lhs = jnp.concatenate(lhs, axis=1)
                rhs = jnp.concatenate(rhs, axis=0)
                score = lax.dot_general(lhs, rhs, (((1,), (1,)), ((), ())), preferred_element_type=jnp.float32)
                weight = jnp.exp2(score).reshape(12, 2, 8, WIDE)
                running = jnp.zeros((2, 8, WIDE), jnp.float32)
                moment = jnp.zeros((2, 8, WIDE), jnp.float32)
                for u in range(11, -1, -1):
                    term = weight[u]
                    if u < 3:
                        term = jnp.where(x_of <= u, term, 0.0)
                    if u > 8:
                        term = jnp.where(x_of >= u - 8, term, 0.0)
                    running = running + term
                    if u:
                        moment = moment + running
                running = running * row_mask
                moment = moment * row_mask
                total = jnp.sum(running[0] + running[1], axis=0, keepdims=True)
                moved = running * row_weight
                y_sum = jnp.sum(moved[0] + moved[1], axis=0, keepdims=True)
                x_sum = jnp.sum(moment[0] + moment[1], axis=0, keepdims=True)
                y_mean, x_mean = y_sum / total, x_sum / total
                for half in range(2):
                    keep = (lane8 // 64 == side) & ((lane8 // 32) % 2 == half) & ((lane8 // 4) % 2 == h)
                    cols = slice(LANES * half, LANES * (half + 1))
                    down = jnp.where(keep, gather(jnp.broadcast_to(y_mean[:, cols], (8, LANES)), pick), down)
                    across = jnp.where(keep, gather(jnp.broadcast_to(x_mean[:, cols], (8, LANES)), pick), across)
        down = down - (REACH + sub8).astype(jnp.float32)
        across = across - (REACH + lane8 % 4).astype(jnp.float32)

        whole = jnp.floor(across)
        part = across - whole
        left = lane8 + whole.astype(jnp.int32)
        right = left + 1
        left_weight = jnp.where((left >= 0) & (left < LANES), 1.0 - part, 0.0)
        right_weight = jnp.where((right >= 0) & (right < LANES), part, 0.0)
        left = jnp.clip(left, 0, LANES - 1)
        right = jnp.clip(right, 0, LANES - 1)
        sums = [down, across]
        shift = jnp.where(k == 1, FIELD_HALO - REACH * sections, 0)
        for step in range(-REACH, REACH + 1):
            row_part = jnp.maximum(0.0, 1.0 - jnp.abs(down - step))
            for c in range(2):
                values = f_ref[k - 1, c, pl.ds(8 * i + REACH + step + shift, 8), :]
                mixed = left_weight * gather(values, left) + right_weight * gather(values, right)
                sums[c] = sums[c] + row_part * mixed
        row = sub8 + 8 * i - extra + tile * rows
        inside = (row >= 0) & (row < total_rows)
        for c in range(2):
            f_ref[k, c, pl.ds(pl.multiple_of(8 * i, 8), 8), :] = jnp.where(inside, sums[c], 0.0)

    def advance(k, carry):
        def step(i, carry):
            block(k, i)
            return carry

        lax.fori_loop(0, (rows + 2 * REACH * (sections - k)) // 8, step, 0)
        return carry

    lax.fori_loop(1, sections + 1, advance, 0)
    for k in range(1, sections + 1):
        extra = REACH * (sections - k)
        out_ref[k - 1] = f_ref[k, :, extra : extra + rows, :]


def on_device(images, section_order, prev_field, conv1_weight, conv1_bias, conv2_weight, conv2_bias):
    count = lax.axis_size("tile")
    forward = [(i, i + 1) for i in range(count - 1)]
    backward = [(target, source) for source, target in forward]
    pixel_rows, columns = images.shape[1:]
    sections = section_order.shape[0]
    rows = prev_field.shape[1]
    channels = conv1_weight.shape[0]
    lo = lax.ppermute(images[:, pixel_rows - HALO :], "tile", forward)
    hi = lax.ppermute(images[:, :HALO], "tile", backward)
    flo = lax.ppermute(prev_field[:, rows - FIELD_HALO :], "tile", forward)
    fhi = lax.ppermute(prev_field[:, :FIELD_HALO], "tile", backward)

    slots = WIDE // channels
    taps = jnp.kron(jnp.eye(slots, dtype=jnp.float32), conv1_weight.astype(jnp.float32).T)
    rest = jnp.tile(conv1_bias, slots)
    rounded = []
    for _ in range(3):
        top = lax.reduce_precision(rest, 8, 7)
        rounded.append(top)
        rest = rest - top
    taps = jnp.concatenate([taps, jnp.stack(rounded)], axis=0).astype(jnp.bfloat16)
    w1 = jnp.dot(jnp.asarray(first_layer_selector(), jnp.bfloat16), taps, preferred_element_type=jnp.float32)
    w1 = w1.astype(jnp.bfloat16).reshape(WINDOWS, WIDE, WIDE)
    w2 = jnp.einsum(
        "bdt,toc->bcdo", jnp.asarray(second_layer_selector(), jnp.bfloat16), conv2_weight,
        preferred_element_type=jnp.float32,
    ).astype(jnp.bfloat16).reshape(WIDE, WIDE)
    b2 = jnp.tile(conv2_bias, LANES // channels)[None]
    meta = jnp.concatenate([lax.axis_index("tile").astype(jnp.int32)[None], section_order])

    groups = columns // (4 * WINDOWS)
    span = (rows + 2 * REACH * sections) // 2 + 4
    vmem = pl.BlockSpec(memory_space=pltpu.VMEM)
    return pl.pallas_call(
        functools.partial(kernel, sections, rows, rows * count, channels),
        out_shape=jax.ShapeDtypeStruct((sections, 2, rows, prev_field.shape[2]), jnp.float32),
        in_specs=[pl.BlockSpec(memory_space=pltpu.SMEM)] + [vmem] * 9,
        out_specs=vmem,
        scratch_shapes=[
            pltpu.VMEM((2, 2 * rows + 96, LANES), jnp.float32),
            pltpu.VMEM((groups * span, WIDE), jnp.bfloat16),
            pltpu.VMEM((groups, span + 2 * PAD, LANES), jnp.float32),
            pltpu.VMEM((2, groups, span, LANES), jnp.float32),
            pltpu.VMEM((sections + 1, 16, 2, 2, 2, span + 2 * PAD, LANES), jnp.float32),
            pltpu.VMEM((sections + 1, 2, rows + 2 * FIELD_HALO + 8, LANES), jnp.float32),
        ],
        compiler_params=pltpu.CompilerParams(vmem_limit_bytes=60 * 1024 * 1024),
        name="align",
    )(meta, images, lo, hi, prev_field, flo, fhi, w1, w2, b2)


def solution(mesh):
    in_specs = (P("parts", "tile", None), P("parts"), P("parts", "tile", None), P(), P(), P(), P())
    out_specs = P("parts", None, "tile", None)
    return jax.shard_map(on_device, mesh=mesh, in_specs=in_specs, out_specs=out_specs, check_vma=False)
```

```python
import functools
import math

import jax
import jax.numpy as jnp
import numpy as np
from jax import lax
from jax.experimental import pallas as pl
from jax.experimental.pallas import tpu as pltpu
from jax.sharding import PartitionSpec as P

SHARPNESS = 16.0
REACH = 4
LANES = 128
WIDE = 256
HALO = 32
FIELD_HALO = 16
PITCH = 40
BIAS_LANE = 248
PAD = 8
WINDOWS = 8


def first_layer_lanes():
    lanes = np.full((1, LANES), -WIDE, np.int32)
    for slot in range(8):
        for tap in range(9):
            pixel_row = 2 * (slot // 4) + tap // 3
            start = PITCH * pixel_row if pixel_row < 3 else LANES + PITCH * (pixel_row - 3)
            lanes[0, 9 * slot + tap] = start + 2 * (slot % 4) + tap % 3
    return lanes


def prepare(lanes_ref, c1_ref, b1_ref, c2_ref, b2_ref, w1_ref, w2_ref, bias_ref):
    channels, taps = c1_ref.shape

    def indices(shape):
        return [lax.broadcasted_iota(jnp.int32, shape, axis) for axis in range(2)]

    def ones_where(condition):
        return jnp.where(condition, 1.0, 0.0).astype(jnp.bfloat16)

    def repeated(values, dims):
        return lax.dot_general(values, spread, (dims, ((), ())), preferred_element_type=jnp.float32)

    row, col = indices((channels, WIDE))
    spread = ones_where(col % channels == row)

    def pieces(ref):
        rest = jnp.broadcast_to(ref[...], (8, channels))
        row = lax.broadcasted_iota(jnp.int32, (8, channels), 0)
        total = jnp.zeros((8, channels), jnp.float32)
        for n in range(3):
            top = rest.astype(jnp.bfloat16).astype(jnp.float32)
            total = jnp.where(row == n, top, total)
            rest = rest - top
        return repeated(total.astype(jnp.bfloat16), ((1,), (0,)))

    bias_ref[...] = jnp.broadcast_to(jnp.sum(pieces(b2_ref), axis=0, keepdims=True), (8, WIDE))[:, :LANES]

    by_tap = repeated(c1_ref[...], ((0,), (0,)))
    row, col = indices((LANES, WIDE))
    table = jnp.zeros((LANES, WIDE), jnp.float32)
    slot = col // channels
    for tap in range(taps):
        table = jnp.where(row == taps * slot + tap, by_tap[tap : tap + 1], table)
    bias = pieces(b1_ref)
    for n in range(3):
        table = jnp.where(row == 8 * taps + n, bias[n : n + 1], table)
    table = table.astype(jnp.bfloat16)
    row, col = indices((WIDE, LANES))
    bias_lane = (col >= 8 * taps) & (col < 8 * taps + 3) & (row == BIAS_LANE + col - 8 * taps)
    for window in range(WINDOWS):
        pick = ones_where((row == lanes_ref[...] + 4 * window) | bias_lane)
        w1_ref[window] = jnp.dot(pick, table, preferred_element_type=jnp.float32).astype(jnp.bfloat16)

    row, col = indices((WIDE, WIDE))
    slot_in, slot_out = row // channels, col // channels
    row_out = slot_out // 2
    row_out = jnp.where(row_out == 0, 2, row_out - 2)
    row_step = slot_in // 4 - row_out
    col_step = slot_in % 4 - 1 - slot_out % 2
    near = (jnp.abs(row_step) <= 1) & (jnp.abs(col_step) <= 1)
    tap_at = jnp.where(near, 3 * row_step + col_step + 4, -1)
    table = jnp.zeros((WIDE, WIDE), jnp.float32)
    for tap in range(taps):
        block = repeated(c2_ref[tap], ((0,), (0,)))
        table = jnp.where(tap_at == tap, jnp.concatenate([block] * (WIDE // channels), axis=0), table)
    w2_ref[...] = table.astype(jnp.bfloat16)


def lane_index(shape):
    return lax.broadcasted_iota(jnp.int32, shape, len(shape) - 1)


def kernel(
    sections, rows, total_rows, channels,
    order_ref, img_ref, lo_ref, hi_ref, fld_ref, w1_ref, w2_ref, b2_ref,
    out_ref, z_ref, x_ref, a_ref, o_ref, t_ref, f_ref, s_ref,
):
    groups = a_ref.shape[0]
    span = x_ref.shape[0] // groups
    per = LANES // channels
    lane = lane_index((1, LANES))
    slot = lane // channels
    tile = lax.axis_index("tile")
    pairs_total = total_rows // 2

    z_ref[...] = jnp.zeros_like(z_ref)
    pictures = HALO * (sections + 1)
    f_ref[0, :, FIELD_HALO : FIELD_HALO + rows, :] = fld_ref[...]
    for ref, start in ((lo_ref, 0), (hi_ref, FIELD_HALO + rows)):
        for c in range(2):
            both = ref[pictures + FIELD_HALO * c : pictures + FIELD_HALO * (c + 1), :].astype(jnp.float32)
            f_ref[0, c, start : start + FIELD_HALO, :] = both[:, :LANES] + both[:, LANES:]

    def encode(k, carry):
        extra = REACH * (sections - k)
        section = jnp.where(k == 0, 0, 1 + order_ref[jnp.maximum(k - 1, 0)])
        border = pl.ds(pl.multiple_of(HALO * section, HALO), HALO)
        base = pl.multiple_of(2 * extra, 8)
        for half in range(2):
            cols = slice(LANES * half, LANES * (half + 1))
            z_ref[half, pl.ds(base, HALO), :] = lo_ref[border, cols].astype(jnp.float32)
            z_ref[half, pl.ds(base + HALO, 2 * rows), :] = img_ref[section, :, cols].astype(jnp.float32)
            z_ref[half, pl.ds(base + HALO + 2 * rows, HALO), :] = hi_ref[border, cols].astype(jnp.float32)
        pair = lax.broadcasted_iota(jnp.int32, (span, LANES), 0) + tile * (rows // 2) - 1 - extra // 2
        valid = jnp.where((pair >= 0) & (pair < pairs_total), 1.0, 0.0)

        for group in range(groups):
            side, place = divmod(group, groups // 2)
            pieces = []
            for row in range(5):
                here = z_ref[side, pl.ds(HALO - 5 + row, span, stride=4), :]
                if place == 0 or (place == groups // 2 - 1 and side == 0):
                    if side == 0 and place == 0:
                        here = jnp.where(lane < LANES // 2, here, 0.0)
                    else:
                        other = z_ref[1 - side, pl.ds(HALO - 5 + row, span, stride=4), :]
                        low, high = (here, other) if side == 1 else (other, here)
                        here = jnp.where(lane < LANES // 2, low, high)
                start = PITCH * (row % 3)
                shift = (start - (2 * LANES // groups * place - 3)) % LANES
                pieces.append(pltpu.roll(here, shift, 1))
            left = jnp.where(lane < PITCH, pieces[0], jnp.where(lane < 2 * PITCH, pieces[1], pieces[2]))
            right = jnp.where(lane < PITCH, pieces[3], jnp.where(lane < BIAS_LANE - LANES, pieces[4], valid))
            x_ref[pl.ds(span * group, span), 0:LANES] = (left * valid).astype(jnp.bfloat16)
            x_ref[pl.ds(span * group, span), LANES:WIDE] = (right * valid).astype(jnp.bfloat16)

        def column(xh, carry):
            for part in range(2):
                window = xh + 4 * part
                first = jnp.dot(x_ref[...], w1_ref[window], preferred_element_type=jnp.float32)
                first = jnp.maximum(first, 0.0).reshape(groups, span, WIDE)
                edge = (lane_index((1, 1, WIDE)) // channels) % 4
                group_at = lax.broadcasted_iota(jnp.int32, (groups, 1, WIDE), 0)
                if part == 0:
                    drop = (edge == 0) & (group_at == 0) & (xh == 0)
                else:
                    drop = (edge == 3) & (group_at == groups - 1) & (xh == 3)
                first = jnp.where(drop, 0.0, first)
                first = first.reshape(groups * span, WIDE).astype(jnp.bfloat16)
                second = jnp.dot(first, w2_ref[...], preferred_element_type=jnp.float32)
                second = second.reshape(groups, span, WIDE)
                a_ref[:, PAD : PAD + span, :] = second[:, :, 0:LANES]
                for group in range(groups):
                    above = a_ref[group, PAD - 1 : PAD - 1 + span, :]
                    below = a_ref[group, PAD + 1 : PAD + 1 + span, :]
                    summed = second[group, :, LANES:WIDE] + jnp.where(lane < LANES // 2, above, below)
                    o_ref[part, group] = jnp.tanh(summed + b2_ref[0:1, :]) * valid
            for side in range(2):
                for half in range(2):
                    at = 4 * side + 2 * half
                    s0, s1, s2, s3 = o_ref[0, at], o_ref[1, at], o_ref[0, at + 1], o_ref[1, at + 1]
                    low = lane < LANES // 2
                    even = slot % 2 == 0
                    a0, a2 = jnp.where(low, s0, pltpu.roll(s2, 64, 1)), jnp.where(low, pltpu.roll(s0, 64, 1), s2)
                    a1, a3 = jnp.where(low, s1, pltpu.roll(s3, 64, 1)), jnp.where(low, pltpu.roll(s1, 64, 1), s3)
                    back = LANES - channels
                    c0, c1 = jnp.where(even, a0, pltpu.roll(a1, channels, 1)), jnp.where(even, pltpu.roll(a0, back, 1), a1)
                    c2, c3 = jnp.where(even, a2, pltpu.roll(a3, channels, 1)), jnp.where(even, pltpu.roll(a2, back, 1), a3)
                    for parity, pixel, value in ((0, 0, c0), (0, 1, c1), (1, 0, c2), (1, 1, c3)):
                        t_ref[k, 4 + 2 * xh + pixel, parity, side, half, PAD : PAD + span, :] = value
            return carry

        lax.fori_loop(0, 4, column, 0)

        def surround(at, carry):
            x_low, parity = at // 2, at % 2
            rows_at = slice(PAD, PAD + span)
            order = [(0, 0), (0, 1), (1, 0), (1, 1)]
            left = [pltpu.roll(t_ref[k, 8 + x_low, parity, s, h, rows_at, :], channels, 1) for s, h in order]
            right = [pltpu.roll(t_ref[k, 4 + x_low, parity, s, h, rows_at, :], LANES - channels, 1) for s, h in order]
            for n, (s, h) in enumerate(order):
                before = left[n - 1] if n else jnp.zeros_like(left[0])
                after = right[n + 1] if n < 3 else jnp.zeros_like(right[0])
                t_ref[k, x_low, parity, s, h, rows_at, :] = jnp.where(slot == 0, before, left[n])
                t_ref[k, 12 + x_low, parity, s, h, rows_at, :] = jnp.where(slot == per - 1, after, right[n])
            return carry

        @pl.when(k < sections)
        def _():
            lax.fori_loop(0, 8, surround, 0)

        return carry

    lax.fori_loop(0, sections + 1, encode, 0)

    scale = SHARPNESS / channels * math.log2(math.e)
    sub8 = lax.broadcasted_iota(jnp.int32, (8, LANES), 0)
    lane8 = lane_index((8, LANES))
    wide = lane_index((1, WIDE))
    x_of = (wide // 8) % 4
    y_of = 2 * (wide % 4) + (wide // 4) % 2
    row_at = 2 * lax.broadcasted_iota(jnp.int32, (2, 8, WIDE), 1) + lax.broadcasted_iota(jnp.int32, (2, 8, WIDE), 0)
    row_weight = row_at.astype(jnp.float32)
    row_mask = jnp.where((row_at >= y_of) & (row_at <= y_of + 2 * REACH), 1.0, 0.0)
    pick = channels * ((lane8 // 8) % 4) + 8 * (lane8 % 4) + 4 * (sub8 % 2) + sub8 // 2
    patch = [jnp.where(slot == q, 1.0, 0.0).astype(jnp.bfloat16) for q in range(per)]

    def gather(values, index):
        return jnp.take_along_axis(values, index, axis=1, mode="promise_in_bounds")

    starts = [0]
    for k in range(1, sections + 1):
        starts.append(starts[-1] + pl.cdiv(rows + 2 * REACH * (sections - k), 16))
    blocks = starts[-1]

    def place(t):
        t = jnp.clip(t, 0, blocks - 1)
        k, first = 1, 0
        for n in range(1, sections):
            k = k + jnp.where(t >= starts[n], 1, 0)
            first = jnp.where(t >= starts[n], starts[n], first)
        return k, 2 * (t - first)

    def scores(k, i, side, h):
        lhs, rhs = [], []
        for half in range(2):
            window = t_ref[k - 1, 4 * h : 4 * h + 12, :, side, half, pl.ds(PAD + 1 + 4 * i, 8), :]
            lhs.append(window.reshape(12 * 16, LANES).astype(jnp.bfloat16))
            even = t_ref[k, 4 + 4 * h : 8 + 4 * h, 0, side, half, pl.ds(PAD + 1 + 4 * i, 8), :]
            odd = t_ref[k, 4 + 4 * h : 8 + 4 * h, 1, side, half, pl.ds(PAD - 3 + 4 * i, 8), :]
            current = jnp.where(sub8 < 4, even, odd) * scale
            current = current.reshape(32, LANES).astype(jnp.bfloat16)
            nothing = jnp.zeros_like(current)
            for q in range(per):
                masked = current * patch[q]
                rhs.append(jnp.concatenate([masked, nothing] if half == 0 else [nothing, masked], axis=1))
        lhs = jnp.concatenate(lhs, axis=1)
        rhs = jnp.concatenate(rhs, axis=0)
        return lax.dot_general(lhs, rhs, (((1,), (1,)), ((), ())), preferred_element_type=jnp.float32)

    def means(at):
        running = jnp.zeros((2, 8, WIDE), jnp.float32)
        moment = jnp.zeros((2, 8, WIDE), jnp.float32)
        for u in range(11, -1, -1):
            term = jnp.exp2(s_ref[at, 16 * u : 16 * u + 16, :]).reshape(2, 8, WIDE)
            if u < 3:
                term = jnp.where(x_of <= u, term, 0.0)
            if u > 8:
                term = jnp.where(x_of >= u - 8, term, 0.0)
            running = running + term
            if u:
                moment = moment + running
        running = running * row_mask
        moment = moment * row_mask
        total = jnp.sum(running[0] + running[1], axis=0, keepdims=True)
        moved = running * row_weight
        y_sum = jnp.sum(moved[0] + moved[1], axis=0, keepdims=True)
        x_sum = jnp.sum(moment[0] + moment[1], axis=0, keepdims=True)
        return y_sum / total, x_sum / total

    def compose(k, i, down, across):
        extra = REACH * (sections - k)
        whole = jnp.floor(across)
        part = across - whole
        left = lane8 + whole.astype(jnp.int32)
        right = left + 1
        left_weight = jnp.where((left >= 0) & (left < LANES), 1.0 - part, 0.0)
        right_weight = jnp.where((right >= 0) & (right < LANES), part, 0.0)
        left = jnp.clip(left, 0, LANES - 1)
        right = jnp.clip(right, 0, LANES - 1)
        sums = [down, across]
        shift = jnp.where(k == 1, FIELD_HALO - REACH * sections, 0)
        for step in range(-REACH, REACH + 1):
            row_part = jnp.maximum(0.0, 1.0 - jnp.abs(down - step))
            for c in range(2):
                values = f_ref[k - 1, c, pl.ds(8 * i + REACH + step + shift, 8), :]
                mixed = left_weight * gather(values, left) + right_weight * gather(values, right)
                sums[c] = sums[c] + row_part * mixed
        row = sub8 + 8 * i - extra + tile * rows
        inside = (row >= 0) & (row < total_rows)
        return [jnp.where(inside, value, 0.0) for value in sums]

    def step(t, carry):
        k, i = place(t)
        k_last, i_last = place(t - 2)
        found = []
        for n in range(2):
            down = jnp.zeros((8, LANES), jnp.float32)
            across = jnp.zeros((8, LANES), jnp.float32)
            for side in range(2):
                for h in range(2):
                    at = 4 * n + 2 * side + h
                    y_mean, x_mean = means(at)
                    s_ref[at] = scores(k, i + n, side, h)
                    for half in range(2):
                        keep = (lane8 // 64 == side) & ((lane8 // 32) % 2 == half) & ((lane8 // 4) % 2 == h)
                        cols = slice(LANES * half, LANES * (half + 1))
                        down = jnp.where(keep, gather(jnp.broadcast_to(y_mean[:, cols], (8, LANES)), pick), down)
                        across = jnp.where(keep, gather(jnp.broadcast_to(x_mean[:, cols], (8, LANES)), pick), across)
            found.append(down - (REACH + sub8).astype(jnp.float32))
            found.append(across - (REACH + lane8 % 4).astype(jnp.float32))
        fields = [compose(k_last, i_last + n, carry[2 * n], carry[2 * n + 1]) for n in range(2)]
        for n in range(2):
            for c in range(2):
                f_ref[k_last, c, pl.ds(pl.multiple_of(8 * i_last + 8 * n, 8), 8), :] = fields[n][c]
        return tuple(found)

    s_ref[...] = jnp.zeros_like(s_ref)
    lax.fori_loop(0, blocks + 2, step, (jnp.zeros((8, LANES), jnp.float32),) * 4)
    for k in range(1, sections + 1):
        extra = REACH * (sections - k)
        out_ref[k - 1] = f_ref[k, :, extra : extra + rows, :]


def on_device(images, section_order, prev_field, conv1_weight, conv1_bias, conv2_weight, conv2_bias):
    count = lax.axis_size("tile")
    forward = [(i, i + 1) for i in range(count - 1)]
    backward = [(target, source) for source, target in forward]
    pixel_rows, columns = images.shape[1:]
    sections = section_order.shape[0]
    rows = prev_field.shape[1]
    channels = conv1_weight.shape[0]

    def packed(picture, field):
        high = lax.reduce_precision(field, 8, 7)
        field = jnp.concatenate([high, field - high], axis=2).astype(jnp.bfloat16)
        return jnp.concatenate([picture.reshape(-1, columns), field.reshape(-1, columns)], axis=0)

    lo = lax.ppermute(packed(images[:, pixel_rows - HALO :], prev_field[:, rows - FIELD_HALO :]), "tile", forward)
    hi = lax.ppermute(packed(images[:, :HALO], prev_field[:, :FIELD_HALO]), "tile", backward)

    vmem = pl.BlockSpec(memory_space=pltpu.VMEM)
    w1, w2, b2 = pl.pallas_call(
        prepare,
        out_shape=(
            jax.ShapeDtypeStruct((WINDOWS, WIDE, WIDE), jnp.bfloat16),
            jax.ShapeDtypeStruct((WIDE, WIDE), jnp.bfloat16),
            jax.ShapeDtypeStruct((8, LANES), jnp.float32),
        ),
        in_specs=[vmem] * 5,
        out_specs=(vmem,) * 3,
        cost_estimate=pl.CostEstimate(flops=10**9, bytes_accessed=10**6, transcendentals=0),
        name="weights",
    )(jnp.asarray(first_layer_lanes()), conv1_weight, conv1_bias[None], conv2_weight, conv2_bias[None])

    groups = columns // (4 * WINDOWS)
    span = (rows + 2 * REACH * sections) // 2 + 4
    return pl.pallas_call(
        functools.partial(kernel, sections, rows, rows * count, channels),
        out_shape=jax.ShapeDtypeStruct((sections, 2, rows, prev_field.shape[2]), jnp.float32),
        in_specs=[pl.BlockSpec(memory_space=pltpu.SMEM)] + [vmem] * 7,
        out_specs=vmem,
        scratch_shapes=[
            pltpu.VMEM((2, 2 * rows + 96, LANES), jnp.float32),
            pltpu.VMEM((groups * span, WIDE), jnp.bfloat16),
            pltpu.VMEM((groups, span + 2 * PAD, LANES), jnp.float32),
            pltpu.VMEM((2, groups, span, LANES), jnp.float32),
            pltpu.VMEM((sections + 1, 16, 2, 2, 2, span + 2 * PAD, LANES), jnp.float32),
            pltpu.VMEM((sections + 1, 2, rows + 2 * FIELD_HALO + 8, LANES), jnp.float32),
            pltpu.VMEM((8, 192, WIDE), jnp.float32),
        ],
        compiler_params=pltpu.CompilerParams(vmem_limit_bytes=60 * 1024 * 1024),
        name="align",
    )(section_order, images, lo, hi, prev_field, w1, w2, b2)


def solution(mesh):
    in_specs = (P("parts", "tile", None), P("parts"), P("parts", "tile", None), P(), P(), P(), P())
    out_specs = P("parts", None, "tile", None)
    return jax.shard_map(on_device, mesh=mesh, in_specs=in_specs, out_specs=out_specs, check_vma=False)
```

```python
import functools
import math

import jax
import jax.numpy as jnp
import numpy as np
from jax import lax
from jax.experimental import pallas as pl
from jax.experimental.pallas import tpu as pltpu
from jax.sharding import PartitionSpec as P

SHARPNESS = 16.0
REACH = 4
LANES = 128
WIDE = 256
HALO = 32
FIELD_HALO = 16
PITCH = 40
BIAS_LANE = 248
PAD = 8
WINDOWS = 8


def first_layer_lanes():
    lanes = np.full((1, LANES), -WIDE, np.int32)
    for slot in range(8):
        for tap in range(9):
            pixel_row = 2 * (slot // 4) + tap // 3
            start = PITCH * pixel_row if pixel_row < 3 else LANES + PITCH * (pixel_row - 3)
            lanes[0, 9 * slot + tap] = start + 2 * (slot % 4) + tap % 3
    return lanes


def prepare(lanes_ref, c1_ref, b1_ref, c2_ref, b2_ref, w1_ref, w2_ref, bias_ref):
    channels, taps = c1_ref.shape

    def indices(shape):
        return [lax.broadcasted_iota(jnp.int32, shape, axis) for axis in range(2)]

    def ones_where(condition):
        return jnp.where(condition, 1.0, 0.0).astype(jnp.bfloat16)

    def repeated(values, dims):
        return lax.dot_general(values, spread, (dims, ((), ())), preferred_element_type=jnp.float32)

    row, col = indices((channels, WIDE))
    spread = ones_where(col % channels == row)

    def pieces(ref):
        rest = jnp.broadcast_to(ref[...], (8, channels))
        row = lax.broadcasted_iota(jnp.int32, (8, channels), 0)
        total = jnp.zeros((8, channels), jnp.float32)
        for n in range(3):
            top = rest.astype(jnp.bfloat16).astype(jnp.float32)
            total = jnp.where(row == n, top, total)
            rest = rest - top
        return repeated(total.astype(jnp.bfloat16), ((1,), (0,)))

    bias_ref[...] = jnp.broadcast_to(jnp.sum(pieces(b2_ref), axis=0, keepdims=True), (8, WIDE))[:, :LANES]

    by_tap = repeated(c1_ref[...], ((0,), (0,)))
    row, col = indices((LANES, WIDE))
    table = jnp.zeros((LANES, WIDE), jnp.float32)
    slot = col // channels
    for tap in range(taps):
        table = jnp.where(row == taps * slot + tap, by_tap[tap : tap + 1], table)
    bias = pieces(b1_ref)
    for n in range(3):
        table = jnp.where(row == 8 * taps + n, bias[n : n + 1], table)
    table = table.astype(jnp.bfloat16)
    row, col = indices((WIDE, LANES))
    bias_lane = (col >= 8 * taps) & (col < 8 * taps + 3) & (row == BIAS_LANE + col - 8 * taps)
    for window in range(WINDOWS):
        pick = ones_where((row == lanes_ref[...] + 4 * window) | bias_lane)
        w1_ref[window] = jnp.dot(pick, table, preferred_element_type=jnp.float32).astype(jnp.bfloat16)

    row, col = indices((WIDE, WIDE))
    slot_in, slot_out = row // channels, col // channels
    row_out = slot_out // 2
    row_out = jnp.where(row_out == 0, 2, row_out - 2)
    row_step = slot_in // 4 - row_out
    col_step = slot_in % 4 - 1 - slot_out % 2
    near = (jnp.abs(row_step) <= 1) & (jnp.abs(col_step) <= 1)
    tap_at = jnp.where(near, 3 * row_step + col_step + 4, -1)
    table = jnp.zeros((WIDE, WIDE), jnp.float32)
    for tap in range(taps):
        block = repeated(c2_ref[tap], ((0,), (0,)))
        table = jnp.where(tap_at == tap, jnp.concatenate([block] * (WIDE // channels), axis=0), table)
    table = table.astype(jnp.bfloat16)
    for skew in range(LANES // channels):
        for half in range(2):
            cols = slice(LANES * half, LANES * (half + 1))
            part = table[:, cols]
            w2_ref[skew, :, cols] = pltpu.roll(part, channels * skew, 1) if skew else part


def lane_index(shape):
    return lax.broadcasted_iota(jnp.int32, shape, len(shape) - 1)


def kernel(
    sections, rows, total_rows, channels,
    order_ref, img_ref, lo_ref, hi_ref, fld_ref, w1_ref, w2_ref, b2_ref,
    out_ref, z_ref, x_ref, p0_ref, p1_ref, t_ref, f_ref, s_ref,
):
    groups = p0_ref.shape[1]
    span = x_ref.shape[0] // groups
    per = LANES // channels
    lane = lane_index((1, LANES))
    slot = lane // channels
    tile = lax.axis_index("tile")
    pairs_total = total_rows // 2

    z_ref[...] = jnp.zeros_like(z_ref)
    pictures = HALO * (sections + 1)
    f_ref[0, :, FIELD_HALO : FIELD_HALO + rows, :] = fld_ref[...]
    for ref, start in ((lo_ref, 0), (hi_ref, FIELD_HALO + rows)):
        for c in range(2):
            both = ref[pictures + FIELD_HALO * c : pictures + FIELD_HALO * (c + 1), :].astype(jnp.float32)
            f_ref[0, c, start : start + FIELD_HALO, :] = both[:, :LANES] + both[:, LANES:]

    def inside_mask(k):
        pair = lax.broadcasted_iota(jnp.int32, (span, LANES), 0) + tile * (rows // 2) - 1
        pair = pair - REACH * (sections - k) // 2
        return jnp.where((pair >= 0) & (pair < pairs_total), 1.0, 0.0)

    def layers(xh, target):
        for part in range(2):
            first = jnp.dot(x_ref[...], w1_ref[xh + 4 * part], preferred_element_type=jnp.float32)
            first = jnp.maximum(first, 0.0)
            edge = (lane_index((1, WIDE)) // channels) % 4
            if xh == 0 and part == 0:
                first = jnp.concatenate([jnp.where(edge == 0, 0.0, first[:span]), first[span:]], axis=0)
            if xh == 3 and part == 1:
                first = jnp.concatenate([first[:-span], jnp.where(edge == 3, 0.0, first[-span:])], axis=0)
            first = first.astype(jnp.bfloat16)
            for odd in range(2):
                half = groups * span // 2
                second = jnp.dot(
                    first[half * odd : half * (odd + 1)], w2_ref[part + 2 * odd], preferred_element_type=jnp.float32
                )
                at = groups // 2 * odd
                target[part, at : at + groups // 2, PAD : PAD + span, :] = second.reshape(groups // 2, span, WIDE)

    def features(k, xh, source):
        valid = inside_mask(k)
        for side in range(2):
            for half in range(2):
                parts = []
                for q in range(per):
                    part, odd = q % 2, q // 2
                    at = (source, part, 2 * side + half + 4 * odd)
                    above = at[0][at[1], at[2], PAD - 1 : PAD - 1 + span, 0:LANES]
                    below = at[0][at[1], at[2], PAD + 1 : PAD + 1 + span, 0:LANES]
                    here = at[0][at[1], at[2], PAD : PAD + span, LANES:WIDE]
                    summed = here + jnp.where((slot + per - q) % per < 2, above, below)
                    parts.append(jnp.tanh(summed + b2_ref[0:1, :]) * valid)
                for t in range(per):
                    value = parts[0]
                    for q in range(1, per):
                        value = jnp.where(slot == (t + q) % per, parts[q], value)

                    def turned(by):
                        by = channels * (by - t) % LANES
                        return pltpu.roll(value, by, 1) if by else value

                    parity, pixel = t // 2, t % 2
                    column = 2 * xh + pixel
                    lines = slice(PAD, PAD + span)
                    t_ref[k, 4 + column, parity, side, half, lines, :] = turned(0)
                    n = 2 * side + half
                    step, edge, border = (1, 0, column - 4) if xh >= 2 else (-1, per - 1, 12 + column)
                    moved = turned(step)
                    own = t_ref.at[k, border, parity, side, half, lines, :]
                    if 0 <= n + step < 4:
                        other = t_ref.at[k, border, parity, (n + step) // 2, (n + step) % 2, lines, :]
                        pltpu.store(other, moved, mask=jnp.broadcast_to(slot == edge, moved.shape))
                    if 0 <= n - step < 4:
                        pltpu.store(own, moved, mask=jnp.broadcast_to(slot != edge, moved.shape))
                    else:
                        own[...] = jnp.where(slot == edge, 0.0, moved)

    def encode(k, carry):
        extra = REACH * (sections - k)
        section = jnp.where(k == 0, 0, 1 + order_ref[jnp.maximum(k - 1, 0)])
        border = pl.ds(pl.multiple_of(HALO * section, HALO), HALO)
        base = pl.multiple_of(2 * extra, 8)
        for half in range(2):
            cols = slice(LANES * half, LANES * (half + 1))
            z_ref[half, pl.ds(base, HALO), :] = lo_ref[border, cols].astype(jnp.float32)
            z_ref[half, pl.ds(base + HALO, 2 * rows), :] = img_ref[section, :, cols].astype(jnp.float32)
            z_ref[half, pl.ds(base + HALO + 2 * rows, HALO), :] = hi_ref[border, cols].astype(jnp.float32)
        valid = inside_mask(k)
        for group in range(groups):
            side, place = divmod(group, groups // 2)
            at = group // 2 + groups // 2 * (group % 2)
            pieces = []
            for row in range(5):
                here = z_ref[side, pl.ds(HALO - 5 + row, span, stride=4), :]
                if place == 0 or (place == groups // 2 - 1 and side == 0):
                    if side == 0 and place == 0:
                        here = jnp.where(lane < LANES // 2, here, 0.0)
                    else:
                        other = z_ref[1 - side, pl.ds(HALO - 5 + row, span, stride=4), :]
                        low, high = (here, other) if side == 1 else (other, here)
                        here = jnp.where(lane < LANES // 2, low, high)
                start = PITCH * (row % 3)
                shift = (start - (2 * LANES // groups * place - 3)) % LANES
                pieces.append(pltpu.roll(here.astype(jnp.bfloat16), shift, 1))
            left = jnp.where(lane < PITCH, pieces[0], jnp.where(lane < 2 * PITCH, pieces[1], pieces[2]))
            right = jnp.where(lane < PITCH, pieces[3], jnp.where(lane < BIAS_LANE - LANES, pieces[4], valid.astype(jnp.bfloat16)))
            x_ref[pl.ds(span * at, span), 0:LANES] = left * valid.astype(jnp.bfloat16)
            x_ref[pl.ds(span * at, span), LANES:WIDE] = right * valid.astype(jnp.bfloat16)

        buffers = (p0_ref, p1_ref)
        for xh in range(4):
            layers(xh, buffers[xh % 2])
            features(k if xh else jnp.maximum(k - 1, 0), (xh - 1) % 4, buffers[(xh - 1) % 2])
        return carry

    lax.fori_loop(0, sections + 1, encode, 0)
    features(sections, 3, p1_ref)

    scale = SHARPNESS / channels * math.log2(math.e)
    sub8 = lax.broadcasted_iota(jnp.int32, (8, LANES), 0)
    lane8 = lane_index((8, LANES))
    wide = lane_index((1, WIDE))
    x_of = (wide // 8) % 4
    y_of = 2 * (wide % 4) + (wide // 4) % 2
    row_at = 2 * lax.broadcasted_iota(jnp.int32, (2, 8, WIDE), 1) + lax.broadcasted_iota(jnp.int32, (2, 8, WIDE), 0)
    row_weight = row_at.astype(jnp.float32)
    row_mask = jnp.where((row_at >= y_of) & (row_at <= y_of + 2 * REACH), 1.0, 0.0)
    pick = channels * ((lane8 // 8) % 4) + 8 * (lane8 % 4) + 4 * (sub8 % 2) + sub8 // 2
    patch = [jnp.where(slot == q, 1.0, 0.0).astype(jnp.bfloat16) for q in range(per)]

    def gather(values, index):
        return jnp.take_along_axis(values, index, axis=1, mode="promise_in_bounds")

    starts = [0]
    for k in range(1, sections + 1):
        starts.append(starts[-1] + pl.cdiv(rows + 2 * REACH * (sections - k), 16))
    blocks = starts[-1]

    def place(t):
        t = jnp.clip(t, 0, blocks - 1)
        k, first = 1, 0
        for n in range(1, sections):
            k = k + jnp.where(t >= starts[n], 1, 0)
            first = jnp.where(t >= starts[n], starts[n], first)
        return k, 2 * (t - first)

    def scores(k, i, side, h):
        lhs, rhs = [], []
        for half in range(2):
            window = t_ref[k - 1, 4 * h : 4 * h + 12, :, side, half, pl.ds(PAD + 1 + 4 * i, 8), :]
            lhs.append(window.reshape(12 * 16, LANES).astype(jnp.bfloat16))
            even = t_ref[k, 4 + 4 * h : 8 + 4 * h, 0, side, half, pl.ds(PAD + 1 + 4 * i, 8), :]
            odd = t_ref[k, 4 + 4 * h : 8 + 4 * h, 1, side, half, pl.ds(PAD - 3 + 4 * i, 8), :]
            current = jnp.where(sub8 < 4, even, odd) * scale
            current = current.reshape(32, LANES).astype(jnp.bfloat16)
            nothing = jnp.zeros_like(current)
            for q in range(per):
                masked = current * patch[q]
                rhs.append(jnp.concatenate([masked, nothing] if half == 0 else [nothing, masked], axis=1))
        lhs = jnp.concatenate(lhs, axis=1)
        rhs = jnp.concatenate(rhs, axis=0)
        return lax.dot_general(lhs, rhs, (((1,), (1,)), ((), ())), preferred_element_type=jnp.float32)

    def means(at):
        running = jnp.zeros((2, 8, WIDE), jnp.float32)
        moment = jnp.zeros((2, 8, WIDE), jnp.float32)
        for u in range(11, -1, -1):
            term = jnp.exp2(s_ref[at, 16 * u : 16 * u + 16, :]).reshape(2, 8, WIDE)
            if u < 3:
                term = jnp.where(x_of <= u, term, 0.0)
            if u > 8:
                term = jnp.where(x_of >= u - 8, term, 0.0)
            running = running + term
            if u:
                moment = moment + running
        running = running * row_mask
        moment = moment * row_mask
        total = jnp.sum(running[0] + running[1], axis=0, keepdims=True)
        moved = running * row_weight
        y_sum = jnp.sum(moved[0] + moved[1], axis=0, keepdims=True)
        x_sum = jnp.sum(moment[0] + moment[1], axis=0, keepdims=True)
        return y_sum / total, x_sum / total

    def compose(k, i, down, across):
        extra = REACH * (sections - k)
        whole = jnp.floor(across)
        part = across - whole
        left = lane8 + whole.astype(jnp.int32)
        right = left + 1
        left_weight = jnp.where((left >= 0) & (left < LANES), 1.0 - part, 0.0)
        right_weight = jnp.where((right >= 0) & (right < LANES), part, 0.0)
        left = jnp.clip(left, 0, LANES - 1)
        right = jnp.clip(right, 0, LANES - 1)
        sums = [down, across]
        shift = jnp.where(k == 1, FIELD_HALO - REACH * sections, 0)
        for step in range(-REACH, REACH + 1):
            row_part = jnp.maximum(0.0, 1.0 - jnp.abs(down - step))
            for c in range(2):
                values = f_ref[k - 1, c, pl.ds(8 * i + REACH + step + shift, 8), :]
                mixed = left_weight * gather(values, left) + right_weight * gather(values, right)
                sums[c] = sums[c] + row_part * mixed
        row = sub8 + 8 * i - extra + tile * rows
        inside = (row >= 0) & (row < total_rows)
        return [jnp.where(inside, value, 0.0) for value in sums]

    def step(t, carry):
        k, i = place(t)
        k_last, i_last = place(t - 2)
        found = []
        for n in range(2):
            down = jnp.zeros((8, LANES), jnp.float32)
            across = jnp.zeros((8, LANES), jnp.float32)
            for side in range(2):
                for h in range(2):
                    at = 4 * n + 2 * side + h
                    y_mean, x_mean = means(at)
                    s_ref[at] = scores(k, i + n, side, h)
                    for half in range(2):
                        keep = (lane8 // 64 == side) & ((lane8 // 32) % 2 == half) & ((lane8 // 4) % 2 == h)
                        cols = slice(LANES * half, LANES * (half + 1))
                        down = jnp.where(keep, gather(jnp.broadcast_to(y_mean[:, cols], (8, LANES)), pick), down)
                        across = jnp.where(keep, gather(jnp.broadcast_to(x_mean[:, cols], (8, LANES)), pick), across)
            found.append(down - (REACH + sub8).astype(jnp.float32))
            found.append(across - (REACH + lane8 % 4).astype(jnp.float32))
        fields = [compose(k_last, i_last + n, carry[2 * n], carry[2 * n + 1]) for n in range(2)]
        for n in range(2):
            for c in range(2):
                f_ref[k_last, c, pl.ds(pl.multiple_of(8 * i_last + 8 * n, 8), 8), :] = fields[n][c]
        return tuple(found)

    s_ref[...] = jnp.zeros_like(s_ref)
    lax.fori_loop(0, blocks + 2, step, (jnp.zeros((8, LANES), jnp.float32),) * 4)
    for k in range(1, sections + 1):
        extra = REACH * (sections - k)
        out_ref[k - 1] = f_ref[k, :, extra : extra + rows, :]


def on_device(images, section_order, prev_field, conv1_weight, conv1_bias, conv2_weight, conv2_bias):
    count = lax.axis_size("tile")
    forward = [(i, i + 1) for i in range(count - 1)]
    backward = [(target, source) for source, target in forward]
    pixel_rows, columns = images.shape[1:]
    sections = section_order.shape[0]
    rows = prev_field.shape[1]
    channels = conv1_weight.shape[0]

    def packed(picture, field):
        high = lax.reduce_precision(field, 8, 7)
        field = jnp.concatenate([high, field - high], axis=2).astype(jnp.bfloat16)
        return jnp.concatenate([picture.reshape(-1, columns), field.reshape(-1, columns)], axis=0)

    lo = lax.ppermute(packed(images[:, pixel_rows - HALO :], prev_field[:, rows - FIELD_HALO :]), "tile", forward)
    hi = lax.ppermute(packed(images[:, :HALO], prev_field[:, :FIELD_HALO]), "tile", backward)

    vmem = pl.BlockSpec(memory_space=pltpu.VMEM)
    w1, w2, b2 = pl.pallas_call(
        prepare,
        out_shape=(
            jax.ShapeDtypeStruct((WINDOWS, WIDE, WIDE), jnp.bfloat16),
            jax.ShapeDtypeStruct((LANES // channels, WIDE, WIDE), jnp.bfloat16),
            jax.ShapeDtypeStruct((8, LANES), jnp.float32),
        ),
        in_specs=[vmem] * 5,
        out_specs=(vmem,) * 3,
        cost_estimate=pl.CostEstimate(flops=10**9, bytes_accessed=10**6, transcendentals=0),
        name="weights",
    )(jnp.asarray(first_layer_lanes()), conv1_weight, conv1_bias[None], conv2_weight, conv2_bias[None])

    groups = columns // (4 * WINDOWS)
    span = (rows + 2 * REACH * sections) // 2 + 4
    return pl.pallas_call(
        functools.partial(kernel, sections, rows, rows * count, channels),
        out_shape=jax.ShapeDtypeStruct((sections, 2, rows, prev_field.shape[2]), jnp.float32),
        in_specs=[pl.BlockSpec(memory_space=pltpu.SMEM)] + [vmem] * 7,
        out_specs=vmem,
        scratch_shapes=[
            pltpu.VMEM((2, 2 * rows + 96, LANES), jnp.float32),
            pltpu.VMEM((groups * span, WIDE), jnp.bfloat16),
            pltpu.VMEM((2, groups, span + 2 * PAD, WIDE), jnp.float32),
            pltpu.VMEM((2, groups, span + 2 * PAD, WIDE), jnp.float32),
            pltpu.VMEM((sections + 1, 16, 2, 2, 2, span + 2 * PAD, LANES), jnp.float32),
            pltpu.VMEM((sections + 1, 2, rows + 2 * FIELD_HALO + 8, LANES), jnp.float32),
            pltpu.VMEM((8, 192, WIDE), jnp.float32),
        ],
        compiler_params=pltpu.CompilerParams(vmem_limit_bytes=60 * 1024 * 1024),
        name="align",
    )(section_order, images, lo, hi, prev_field, w1, w2, b2)


def solution(mesh):
    in_specs = (P("parts", "tile", None), P("parts"), P("parts", "tile", None), P(), P(), P(), P())
    out_specs = P("parts", None, "tile", None)
    return jax.shard_map(on_device, mesh=mesh, in_specs=in_specs, out_specs=out_specs, check_vma=False)
```

```python
import functools
import math

import jax
import jax.numpy as jnp
import numpy as np
from jax import lax
from jax.experimental import pallas as pl
from jax.experimental.pallas import tpu as pltpu
from jax.sharding import PartitionSpec as P

SHARPNESS = 16.0
REACH = 4
LANES = 128
WIDE = 256
HALO = 32
LATER = 24
FIELD_HALO = 16
PITCH = 40
BIAS_LANE = 248
PAD = 8
WINDOWS = 8


def first_layer_lanes():
    lanes = np.full((1, LANES), -WIDE, np.int32)
    for slot in range(8):
        for tap in range(9):
            pixel_row = 2 * (slot // 4) + tap // 3
            start = PITCH * pixel_row if pixel_row < 3 else LANES + PITCH * (pixel_row - 3)
            lanes[0, 9 * slot + tap] = start + 2 * (slot % 4) + tap % 3
    return lanes


def pack(img_ref, fld_ref, up_ref, down_ref, field_ref, sem):
    sections = img_ref.shape[0] - 1
    copies = []
    for side, out_ref in enumerate((up_ref, down_ref)):
        at = 0
        for section in range(sections + 1):
            count = LATER if section else HALO
            first = 0 if side else img_ref.shape[1] - count
            copies.append(
                pltpu.make_async_copy(
                    img_ref.at[section, first : first + count], out_ref.at[at : at + count], sem.at[side, section]
                )
            )
            at += count
        first = 0 if side else fld_ref.shape[1] - FIELD_HALO
        copies.append(
            pltpu.make_async_copy(
                fld_ref.at[:, first : first + FIELD_HALO], field_ref.at[side], sem.at[side, sections + 1]
            )
        )
    for copy in copies:
        copy.start()
    for copy in copies:
        copy.wait()
    for side, out_ref in enumerate((up_ref, down_ref)):
        field = jnp.concatenate([field_ref[side, 0], field_ref[side, 1]], axis=1)
        out_ref[HALO + LATER * sections :, :] = field.astype(jnp.bfloat16)


def prepare(chain_ref, lanes_ref, c1_ref, b1_ref, c2_ref, b2_ref, w1_ref, w2_ref, bias_ref):
    del chain_ref
    channels, taps = c1_ref.shape

    def indices(shape):
        return [lax.broadcasted_iota(jnp.int32, shape, axis) for axis in range(2)]

    def ones_where(condition):
        return jnp.where(condition, 1.0, 0.0).astype(jnp.bfloat16)

    def repeated(values, dims):
        return lax.dot_general(values, spread, (dims, ((), ())), preferred_element_type=jnp.float32)

    row, col = indices((channels, WIDE))
    spread = ones_where(col % channels == row)

    def pieces(ref):
        rest = jnp.broadcast_to(ref[...], (8, channels))
        row = lax.broadcasted_iota(jnp.int32, (8, channels), 0)
        total = jnp.zeros((8, channels), jnp.float32)
        for n in range(3):
            top = rest.astype(jnp.bfloat16).astype(jnp.float32)
            total = jnp.where(row == n, top, total)
            rest = rest - top
        return repeated(total.astype(jnp.bfloat16), ((1,), (0,)))

    bias_ref[...] = jnp.broadcast_to(jnp.sum(pieces(b2_ref), axis=0, keepdims=True), (8, WIDE))[:, :LANES]

    by_tap = repeated(c1_ref[...], ((0,), (0,)))
    row, col = indices((LANES, WIDE))
    table = jnp.zeros((LANES, WIDE), jnp.float32)
    slot = col // channels
    for tap in range(taps):
        table = jnp.where(row == taps * slot + tap, by_tap[tap : tap + 1], table)
    bias = pieces(b1_ref)
    for n in range(3):
        table = jnp.where(row == 8 * taps + n, bias[n : n + 1], table)
    table = table.astype(jnp.bfloat16)
    row, col = indices((WIDE, LANES))
    bias_lane = (col >= 8 * taps) & (col < 8 * taps + 3) & (row == BIAS_LANE + col - 8 * taps)
    for window in range(WINDOWS):
        pick = ones_where((row == lanes_ref[...] + 4 * window) | bias_lane)
        w1_ref[window] = jnp.dot(pick, table, preferred_element_type=jnp.float32).astype(jnp.bfloat16)

    row, col = indices((WIDE, WIDE))
    slot_in, slot_out = row // channels, col // channels
    row_out = slot_out // 2
    row_out = jnp.where(row_out == 0, 2, row_out - 2)
    row_step = slot_in // 4 - row_out
    col_step = slot_in % 4 - 1 - slot_out % 2
    near = (jnp.abs(row_step) <= 1) & (jnp.abs(col_step) <= 1)
    tap_at = jnp.where(near, 3 * row_step + col_step + 4, -1)
    table = jnp.zeros((WIDE, WIDE), jnp.float32)
    for tap in range(taps):
        block = repeated(c2_ref[tap], ((0,), (0,)))
        table = jnp.where(tap_at == tap, jnp.concatenate([block] * (WIDE // channels), axis=0), table)
    table = table.astype(jnp.bfloat16)
    for skew in range(LANES // channels):
        for half in range(2):
            cols = slice(LANES * half, LANES * (half + 1))
            part = table[:, cols]
            w2_ref[skew, :, cols] = pltpu.roll(part, channels * skew, 1) if skew else part


def lane_index(shape):
    return lax.broadcasted_iota(jnp.int32, shape, len(shape) - 1)


def kernel(
    sections, rows, total_rows, channels,
    chain_ref, img_ref, lo_ref, hi_ref, fld_ref, w1_ref, w2_ref, b2_ref,
    out_ref, z_ref, x_ref, p0_ref, p1_ref, t_ref, f_ref, s0_ref, s1_ref,
):
    groups = p0_ref.shape[1]
    span = x_ref.shape[0] // groups
    per = LANES // channels
    lane = lane_index((1, LANES))
    slot = lane // channels
    tile = lax.axis_index("tile")
    pairs_total = total_rows // 2

    z_ref[...] = jnp.zeros_like(z_ref)
    pictures = HALO + LATER * sections
    f_ref[0, :, FIELD_HALO : FIELD_HALO + rows, :] = fld_ref[...]
    for ref, start in ((lo_ref, 0), (hi_ref, FIELD_HALO + rows)):
        for c in range(2):
            part = ref[pictures : pictures + FIELD_HALO, LANES * c : LANES * (c + 1)]
            f_ref[0, c, start : start + FIELD_HALO, :] = part.astype(jnp.float32)

    def inside_mask(k):
        pair = lax.broadcasted_iota(jnp.int32, (span, LANES), 0) + tile * (rows // 2) - 1
        pair = pair - REACH * (sections - k) // 2
        return jnp.where((pair >= 0) & (pair < pairs_total), 1.0, 0.0)

    def layers(xh, target):
        for part in range(2):
            first = jnp.dot(x_ref[...], w1_ref[xh + 4 * part], preferred_element_type=jnp.float32)
            first = jnp.maximum(first, 0.0)
            edge = (lane_index((1, WIDE)) // channels) % 4
            if xh == 0 and part == 0:
                first = jnp.concatenate([jnp.where(edge == 0, 0.0, first[:span]), first[span:]], axis=0)
            if xh == 3 and part == 1:
                first = jnp.concatenate([first[:-span], jnp.where(edge == 3, 0.0, first[-span:])], axis=0)
            first = first.astype(jnp.bfloat16)
            for odd in range(2):
                half = groups * span // 2
                second = jnp.dot(
                    first[half * odd : half * (odd + 1)], w2_ref[part + 2 * odd], preferred_element_type=jnp.float32
                )
                at = groups // 2 * odd
                target[part, at : at + groups // 2, PAD : PAD + span, :] = second.reshape(groups // 2, span, WIDE)

    def features(k, xh, source):
        valid = inside_mask(k)
        for side in range(2):
            for half in range(2):
                parts = []
                for q in range(per):
                    part, odd = q % 2, q // 2
                    at = (source, part, 2 * side + half + 4 * odd)
                    above = at[0][at[1], at[2], PAD - 1 : PAD - 1 + span, 0:LANES]
                    below = at[0][at[1], at[2], PAD + 1 : PAD + 1 + span, 0:LANES]
                    here = at[0][at[1], at[2], PAD : PAD + span, LANES:WIDE]
                    summed = here + jnp.where((slot + per - q) % per < 2, above, below)
                    parts.append(jnp.tanh(summed + b2_ref[0:1, :]) * valid)
                for t in range(per):
                    value = parts[0]
                    for q in range(1, per):
                        value = jnp.where(slot == (t + q) % per, parts[q], value)

                    def turned(by):
                        by = channels * (by - t) % LANES
                        return pltpu.roll(value, by, 1) if by else value

                    parity, pixel = t // 2, t % 2
                    column = 2 * xh + pixel
                    lines = slice(PAD, PAD + span)
                    t_ref[k, 4 + column, parity, side, half, lines, :] = turned(0)
                    n = 2 * side + half
                    step, edge, border = (1, 0, column - 4) if xh >= 2 else (-1, per - 1, 12 + column)
                    moved = turned(step)
                    own = t_ref.at[k, border, parity, side, half, lines, :]
                    if 0 <= n + step < 4:
                        other = t_ref.at[k, border, parity, (n + step) // 2, (n + step) % 2, lines, :]
                        pltpu.store(other, moved, mask=jnp.broadcast_to(slot == edge, moved.shape))
                    if 0 <= n - step < 4:
                        pltpu.store(own, moved, mask=jnp.broadcast_to(slot != edge, moved.shape))
                    else:
                        own[...] = jnp.where(slot == edge, 0.0, moved)

    def encode(k, carry):
        extra = REACH * (sections - k)
        section = jnp.where(k == 0, 0, chain_ref[jnp.maximum(k - 1, 0)])
        first = jnp.where(k == 0, 0, HALO + LATER * (section - 1))
        low = pl.ds(pl.multiple_of(first + jnp.where(k == 0, HALO - LATER, 0), 8), LATER)
        high = pl.ds(pl.multiple_of(first, 8), LATER)
        base = pl.multiple_of(2 * extra + HALO, 8)
        for half in range(2):
            cols = slice(LANES * half, LANES * (half + 1))
            z_ref[half, pl.ds(base - LATER, LATER), :] = lo_ref[low, cols].astype(jnp.float32)
            z_ref[half, pl.ds(base, 2 * rows), :] = img_ref[section, :, cols].astype(jnp.float32)
            z_ref[half, pl.ds(base + 2 * rows, LATER), :] = hi_ref[high, cols].astype(jnp.float32)

        @pl.when(k == 0)
        def _():
            for half in range(2):
                cols = slice(LANES * half, LANES * (half + 1))
                far = HALO - LATER
                z_ref[half, pl.ds(base - HALO, far), :] = lo_ref[0:far, cols].astype(jnp.float32)
                z_ref[half, pl.ds(base + 2 * rows + LATER, far), :] = hi_ref[LATER:HALO, cols].astype(jnp.float32)

        valid = inside_mask(k)
        for group in range(groups):
            side, place = divmod(group, groups // 2)
            at = group // 2 + groups // 2 * (group % 2)
            pieces = []
            for row in range(5):
                here = z_ref[side, pl.ds(HALO - 5 + row, span, stride=4), :]
                if place == 0 or (place == groups // 2 - 1 and side == 0):
                    if side == 0 and place == 0:
                        here = jnp.where(lane < LANES // 2, here, 0.0)
                    else:
                        other = z_ref[1 - side, pl.ds(HALO - 5 + row, span, stride=4), :]
                        low, high = (here, other) if side == 1 else (other, here)
                        here = jnp.where(lane < LANES // 2, low, high)
                start = PITCH * (row % 3)
                shift = (start - (2 * LANES // groups * place - 3)) % LANES
                pieces.append(pltpu.roll(here.astype(jnp.bfloat16), shift, 1))
            left = jnp.where(lane < PITCH, pieces[0], jnp.where(lane < 2 * PITCH, pieces[1], pieces[2]))
            right = jnp.where(lane < PITCH, pieces[3], jnp.where(lane < BIAS_LANE - LANES, pieces[4], valid.astype(jnp.bfloat16)))
            x_ref[pl.ds(span * at, span), 0:LANES] = left * valid.astype(jnp.bfloat16)
            x_ref[pl.ds(span * at, span), LANES:WIDE] = right * valid.astype(jnp.bfloat16)

        buffers = (p0_ref, p1_ref)
        for xh in range(4):
            layers(xh, buffers[xh % 2])
            features(k if xh else jnp.maximum(k - 1, 0), (xh - 1) % 4, buffers[(xh - 1) % 2])
        return carry

    lax.fori_loop(0, sections + 1, encode, 0)
    features(sections, 3, p1_ref)

    scale = SHARPNESS / channels * math.log2(math.e)
    sub8 = lax.broadcasted_iota(jnp.int32, (8, LANES), 0)
    lane8 = lane_index((8, LANES))
    wide = lane_index((1, WIDE))
    x_of = (wide // 8) % 4
    y_of = 2 * (wide % 4) + (wide // 4) % 2
    row_at = 2 * lax.broadcasted_iota(jnp.int32, (2, 8, WIDE), 1) + lax.broadcasted_iota(jnp.int32, (2, 8, WIDE), 0)
    row_weight = row_at.astype(jnp.float32)
    row_mask = jnp.where((row_at >= y_of) & (row_at <= y_of + 2 * REACH), 1.0, 0.0)
    pick = channels * ((lane8 // 8) % 4) + 8 * (lane8 % 4) + 4 * (sub8 % 2) + sub8 // 2
    patch = [jnp.where(slot == q, 1.0, 0.0).astype(jnp.bfloat16) for q in range(per)]

    def gather(values, index):
        return jnp.take_along_axis(values, index, axis=1, mode="promise_in_bounds")

    starts = [0]
    for k in range(1, sections + 1):
        starts.append(starts[-1] + pl.cdiv(rows + 2 * REACH * (sections - k), 16))
    blocks = starts[-1]

    def place(t):
        t = jnp.clip(t, 0, blocks - 1)
        k, first = 1, 0
        for n in range(1, sections):
            k = k + jnp.where(t >= starts[n], 1, 0)
            first = jnp.where(t >= starts[n], starts[n], first)
        return k, 2 * (t - first)

    def scores(k, i, side, h):
        lhs, rhs = [], []
        for half in range(2):
            window = t_ref[k - 1, 4 * h : 4 * h + 12, :, side, half, pl.ds(PAD + 1 + 4 * i, 8), :]
            lhs.append(window.reshape(12 * 16, LANES).astype(jnp.bfloat16))
            even = t_ref[k, 4 + 4 * h : 8 + 4 * h, 0, side, half, pl.ds(PAD + 1 + 4 * i, 8), :]
            odd = t_ref[k, 4 + 4 * h : 8 + 4 * h, 1, side, half, pl.ds(PAD - 3 + 4 * i, 8), :]
            current = jnp.where(sub8 < 4, even, odd) * scale
            current = current.reshape(32, LANES).astype(jnp.bfloat16)
            nothing = jnp.zeros_like(current)
            for q in range(per):
                masked = current * patch[q]
                rhs.append(jnp.concatenate([masked, nothing] if half == 0 else [nothing, masked], axis=1))
        lhs = jnp.concatenate(lhs, axis=1)
        rhs = jnp.concatenate(rhs, axis=0)
        return lax.dot_general(lhs, rhs, (((1,), (1,)), ((), ())), preferred_element_type=jnp.float32)

    def means(source, at):
        running = jnp.zeros((2, 8, WIDE), jnp.float32)
        moment = jnp.zeros((2, 8, WIDE), jnp.float32)
        for u in range(11, -1, -1):
            term = jnp.exp2(source[at, 16 * u : 16 * u + 16, :]).reshape(2, 8, WIDE)
            if u < 3:
                term = jnp.where(x_of <= u, term, 0.0)
            if u > 8:
                term = jnp.where(x_of >= u - 8, term, 0.0)
            running = running + term
            if u:
                moment = moment + running
        running = running * row_mask
        moment = moment * row_mask
        total = jnp.sum(running[0] + running[1], axis=0, keepdims=True)
        moved = running * row_weight
        y_sum = jnp.sum(moved[0] + moved[1], axis=0, keepdims=True)
        x_sum = jnp.sum(moment[0] + moment[1], axis=0, keepdims=True)
        return y_sum / total, x_sum / total

    def compose(k, i, down, across):
        extra = REACH * (sections - k)
        whole = jnp.floor(across)
        part = across - whole
        left = lane8 + whole.astype(jnp.int32)
        right = left + 1
        left_weight = jnp.where((left >= 0) & (left < LANES), 1.0 - part, 0.0)
        right_weight = jnp.where((right >= 0) & (right < LANES), part, 0.0)
        left = jnp.clip(left, 0, LANES - 1)
        right = jnp.clip(right, 0, LANES - 1)
        sums = [down, across]
        shift = jnp.where(k == 1, FIELD_HALO - REACH * sections, 0)
        for step in range(-REACH, REACH + 1):
            row_part = jnp.maximum(0.0, 1.0 - jnp.abs(down - step))
            for c in range(2):
                values = f_ref[k - 1, c, pl.ds(8 * i + REACH + step + shift, 8), :]
                mixed = left_weight * gather(values, left) + right_weight * gather(values, right)
                sums[c] = sums[c] + row_part * mixed
        row = sub8 + 8 * i - extra + tile * rows
        inside = (row >= 0) & (row < total_rows)
        return [jnp.where(inside, value, 0.0) for value in sums]

    def fill(t, target, at):
        k, i = place(t)
        target[at] = scores(k, i + at // 4, at // 2 % 2, at % 2)

    def finish(t, found):
        k, i = place(t)
        fields = [compose(k, i + n, found[2 * n], found[2 * n + 1]) for n in range(2)]
        for n in range(2):
            for c in range(2):
                f_ref[k, c, pl.ds(pl.multiple_of(8 * i + 8 * n, 8), 8), :] = fields[n][c]

    def step(t, carry, source, target):
        found = []
        for n in range(2):
            down = jnp.zeros((8, LANES), jnp.float32)
            across = jnp.zeros((8, LANES), jnp.float32)
            for side in range(2):
                for h in range(2):
                    at = 4 * n + 2 * side + h
                    fill(t + 1, target, at)
                    y_mean, x_mean = means(source, at)
                    for half in range(2):
                        keep = (lane8 // 64 == side) & ((lane8 // 32) % 2 == half) & ((lane8 // 4) % 2 == h)
                        cols = slice(LANES * half, LANES * (half + 1))
                        down = jnp.where(keep, gather(jnp.broadcast_to(y_mean[:, cols], (8, LANES)), pick), down)
                        across = jnp.where(keep, gather(jnp.broadcast_to(x_mean[:, cols], (8, LANES)), pick), across)
            found.append(down - (REACH + sub8).astype(jnp.float32))
            found.append(across - (REACH + lane8 % 4).astype(jnp.float32))
        finish(t - 1, carry)
        return tuple(found)

    def two_steps(j, carry):
        carry = step(2 * j, carry, s0_ref, s1_ref)
        return step(2 * j + 1, carry, s1_ref, s0_ref)

    for at in range(8):
        fill(0, s0_ref, at)
    turns = pl.cdiv(blocks, 2)
    found = lax.fori_loop(0, turns, two_steps, (jnp.zeros((8, LANES), jnp.float32),) * 4)
    finish(2 * turns - 1, found)
    for k in range(1, sections + 1):
        extra = REACH * (sections - k)
        out_ref[k - 1] = f_ref[k, :, extra : extra + rows, :]


def on_device(images, section_order, prev_field, conv1_weight, conv1_bias, conv2_weight, conv2_bias):
    count = lax.axis_size("tile")
    forward = [(i, i + 1) for i in range(count - 1)]
    backward = [(target, source) for source, target in forward]
    pixel_rows, columns = images.shape[1:]
    sections = section_order.shape[0]
    rows = prev_field.shape[1]
    channels = conv1_weight.shape[0]

    vmem = pl.BlockSpec(memory_space=pltpu.VMEM)
    hbm = pl.BlockSpec(memory_space=pl.ANY)
    held = HALO + LATER * sections + FIELD_HALO
    up, down = pl.pallas_call(
        pack,
        out_shape=(jax.ShapeDtypeStruct((held, columns), images.dtype),) * 2,
        in_specs=[hbm, hbm],
        out_specs=(vmem, vmem),
        scratch_shapes=[
            pltpu.VMEM((2, 2, FIELD_HALO, prev_field.shape[2]), jnp.float32),
            pltpu.SemaphoreType.DMA((2, sections + 2)),
        ],
        compiler_params=pltpu.CompilerParams(vmem_limit_bytes=66850000),
        name="pack",
    )(images, prev_field)
    chain = section_order + 1
    lo = lax.ppermute(up, "tile", forward)
    hi = lax.ppermute(down, "tile", backward)

    w1, w2, b2 = pl.pallas_call(
        prepare,
        out_shape=(
            jax.ShapeDtypeStruct((WINDOWS, WIDE, WIDE), jnp.bfloat16),
            jax.ShapeDtypeStruct((LANES // channels, WIDE, WIDE), jnp.bfloat16),
            jax.ShapeDtypeStruct((8, LANES), jnp.float32),
        ),
        in_specs=[pl.BlockSpec(memory_space=pltpu.SMEM)] + [vmem] * 5,
        out_specs=(vmem,) * 3,
        cost_estimate=pl.CostEstimate(flops=10**9, bytes_accessed=10**6, transcendentals=0),
        compiler_params=pltpu.CompilerParams(vmem_limit_bytes=12 * 1024 * 1024),
        name="weights",
    )(chain, jnp.asarray(first_layer_lanes()), conv1_weight, conv1_bias[None], conv2_weight, conv2_bias[None])

    groups = columns // (4 * WINDOWS)
    span = (rows + 2 * REACH * sections) // 2 + 4
    return pl.pallas_call(
        functools.partial(kernel, sections, rows, rows * count, channels),
        out_shape=jax.ShapeDtypeStruct((sections, 2, rows, prev_field.shape[2]), jnp.float32),
        in_specs=[pl.BlockSpec(memory_space=pltpu.SMEM)] + [vmem] * 7,
        out_specs=vmem,
        scratch_shapes=[
            pltpu.VMEM((2, 2 * rows + 96, LANES), jnp.float32),
            pltpu.VMEM((groups * span, WIDE), jnp.bfloat16),
            pltpu.VMEM((2, groups, span + 2 * PAD, WIDE), jnp.float32),
            pltpu.VMEM((2, groups, span + 2 * PAD, WIDE), jnp.float32),
            pltpu.VMEM((sections + 1, 16, 2, 2, 2, span + 2 * PAD, LANES), jnp.float32),
            pltpu.VMEM((sections + 1, 2, rows + 2 * FIELD_HALO + 8, LANES), jnp.float32),
            pltpu.VMEM((8, 192, WIDE), jnp.float32),
            pltpu.VMEM((8, 192, WIDE), jnp.float32),
        ],
        compiler_params=pltpu.CompilerParams(vmem_limit_bytes=44 * 1024 * 1024),
        name="align",
    )(chain, images, lo, hi, prev_field, w1, w2, b2)


def solution(mesh):
    in_specs = (P("parts", "tile", None), P("parts"), P("parts", "tile", None), P(), P(), P(), P())
    out_specs = P("parts", None, "tile", None)
    return jax.shard_map(on_device, mesh=mesh, in_specs=in_specs, out_specs=out_specs, check_vma=False)
```

```python
import functools
import math

import jax
import jax.numpy as jnp
import numpy as np
from jax import lax
from jax.experimental import pallas as pl
from jax.experimental.pallas import tpu as pltpu
from jax.sharding import PartitionSpec as P

SHARPNESS = 16.0
REACH = 4
LANES = 128
WIDE = 256
HALO = 32
LATER = 24
FIELD_HALO = 16
PITCH = 40
BIAS_LANE = 248
PAD = 8
WINDOWS = 8


def first_layer_lanes():
    lanes = np.full((1, LANES), -WIDE, np.int32)
    for slot in range(8):
        for tap in range(9):
            pixel_row = 2 * (slot // 4) + tap // 3
            start = PITCH * pixel_row if pixel_row < 3 else LANES + PITCH * (pixel_row - 3)
            lanes[0, 9 * slot + tap] = start + 2 * (slot % 4) + tap % 3
    return lanes


def pack(img_ref, fld_ref, up_ref, down_ref, field_ref, sem):
    sections = img_ref.shape[0] - 1
    copies = []
    for side, out_ref in enumerate((up_ref, down_ref)):
        at = 0
        for section in range(sections + 1):
            count = LATER if section else HALO
            first = 0 if side else img_ref.shape[1] - count
            copies.append(
                pltpu.make_async_copy(
                    img_ref.at[section, first : first + count], out_ref.at[at : at + count], sem.at[side, section]
                )
            )
            at += count
        first = 0 if side else fld_ref.shape[1] - FIELD_HALO
        copies.append(
            pltpu.make_async_copy(
                fld_ref.at[:, first : first + FIELD_HALO], field_ref.at[side], sem.at[side, sections + 1]
            )
        )
    for copy in copies:
        copy.start()
    for copy in copies:
        copy.wait()
    for side, out_ref in enumerate((up_ref, down_ref)):
        field = jnp.concatenate([field_ref[side, 0], field_ref[side, 1]], axis=1)
        out_ref[HALO + LATER * sections :, :] = field.astype(jnp.bfloat16)


def prepare(chain_ref, lanes_ref, c1_ref, b1_ref, c2_ref, b2_ref, w1_ref, w2_ref, bias_ref):
    del chain_ref
    channels, taps = c1_ref.shape

    def indices(shape):
        return [lax.broadcasted_iota(jnp.int32, shape, axis) for axis in range(2)]

    def ones_where(condition):
        return jnp.where(condition, 1.0, 0.0).astype(jnp.bfloat16)

    def repeated(values, dims):
        return lax.dot_general(values, spread, (dims, ((), ())), preferred_element_type=jnp.float32)

    row, col = indices((channels, WIDE))
    spread = ones_where(col % channels == row)

    def pieces(ref):
        rest = jnp.broadcast_to(ref[...], (8, channels))
        row = lax.broadcasted_iota(jnp.int32, (8, channels), 0)
        total = jnp.zeros((8, channels), jnp.float32)
        for n in range(3):
            top = rest.astype(jnp.bfloat16).astype(jnp.float32)
            total = jnp.where(row == n, top, total)
            rest = rest - top
        return repeated(total.astype(jnp.bfloat16), ((1,), (0,)))

    bias_ref[...] = jnp.broadcast_to(jnp.sum(pieces(b2_ref), axis=0, keepdims=True), (8, WIDE))[:, :LANES]

    by_tap = repeated(c1_ref[...], ((0,), (0,)))
    row, col = indices((LANES, WIDE))
    table = jnp.zeros((LANES, WIDE), jnp.float32)
    slot = col // channels
    for tap in range(taps):
        table = jnp.where(row == taps * slot + tap, by_tap[tap : tap + 1], table)
    bias = pieces(b1_ref)
    for n in range(3):
        table = jnp.where(row == 8 * taps + n, bias[n : n + 1], table)
    table = table.astype(jnp.bfloat16)
    row, col = indices((WIDE, LANES))
    bias_lane = (col >= 8 * taps) & (col < 8 * taps + 3) & (row == BIAS_LANE + col - 8 * taps)
    for window in range(WINDOWS):
        pick = ones_where((row == lanes_ref[...] + 4 * window) | bias_lane)
        w1_ref[window] = jnp.dot(pick, table, preferred_element_type=jnp.float32).astype(jnp.bfloat16)

    row, col = indices((WIDE, WIDE))
    slot_in, slot_out = row // channels, col // channels
    row_out = slot_out // 2
    row_out = jnp.where(row_out == 0, 2, row_out - 2)
    row_step = slot_in // 4 - row_out
    col_step = slot_in % 4 - 1 - slot_out % 2
    near = (jnp.abs(row_step) <= 1) & (jnp.abs(col_step) <= 1)
    tap_at = jnp.where(near, 3 * row_step + col_step + 4, -1)
    table = jnp.zeros((WIDE, WIDE), jnp.float32)
    for tap in range(taps):
        block = repeated(c2_ref[tap], ((0,), (0,)))
        table = jnp.where(tap_at == tap, jnp.concatenate([block] * (WIDE // channels), axis=0), table)
    table = table.astype(jnp.bfloat16)
    for skew in range(LANES // channels):
        for half in range(2):
            cols = slice(LANES * half, LANES * (half + 1))
            part = table[:, cols]
            w2_ref[skew, :, cols] = pltpu.roll(part, channels * skew, 1) if skew else part


def lane_index(shape):
    return lax.broadcasted_iota(jnp.int32, shape, len(shape) - 1)


def kernel(
    sections, rows, total_rows, channels,
    chain_ref, img_ref, lo_ref, hi_ref, fld_ref, w1_ref, w2_ref, b2_ref,
    out_ref, z_ref, x_ref, a0_ref, a1_ref, b0_ref, b1_ref, t_ref, f_ref, s0_ref, s1_ref,
):
    groups = a0_ref.shape[1]
    span = x_ref.shape[0] // groups
    per = LANES // channels
    lane = lane_index((1, LANES))
    slot = lane // channels
    tile = lax.axis_index("tile")
    pairs_total = total_rows // 2

    z_ref[...] = jnp.zeros_like(z_ref)
    pictures = HALO + LATER * sections
    f_ref[0, :, FIELD_HALO : FIELD_HALO + rows, :] = fld_ref[...]
    for ref, start in ((lo_ref, 0), (hi_ref, FIELD_HALO + rows)):
        for c in range(2):
            part = ref[pictures : pictures + FIELD_HALO, LANES * c : LANES * (c + 1)]
            f_ref[0, c, start : start + FIELD_HALO, :] = part.astype(jnp.float32)

    def inside_mask(k):
        pair = lax.broadcasted_iota(jnp.int32, (span, LANES), 0) + tile * (rows // 2) - 1
        pair = pair - REACH * (sections - k) // 2
        return jnp.where((pair >= 0) & (pair < pairs_total), 1.0, 0.0)

    def layers(xh, target):
        for part in range(2):
            first = jnp.dot(x_ref[...], w1_ref[xh + 4 * part], preferred_element_type=jnp.float32)
            first = jnp.maximum(first, 0.0)
            edge = (lane_index((1, WIDE)) // channels) % 4
            if xh == 0 and part == 0:
                first = jnp.concatenate([jnp.where(edge == 0, 0.0, first[:span]), first[span:]], axis=0)
            if xh == 3 and part == 1:
                first = jnp.concatenate([first[:-span], jnp.where(edge == 3, 0.0, first[-span:])], axis=0)
            first = first.astype(jnp.bfloat16)
            for odd in range(2):
                half = groups * span // 2
                second = jnp.dot(
                    first[half * odd : half * (odd + 1)], w2_ref[part + 2 * odd], preferred_element_type=jnp.float32
                )
                at = groups // 2 * odd
                second = second.reshape(groups // 2, span, WIDE)
                target[0][part, at : at + groups // 2, PAD : PAD + span, :] = second[:, :, :LANES]
                target[1][part, at : at + groups // 2] = second[:, :, LANES:]

    def features(k, xh, source):
        valid = inside_mask(k)
        for side in range(2):
            for half in range(2):
                parts = []
                for q in range(per):
                    part, odd = q % 2, q // 2
                    at = 2 * side + half + 4 * odd
                    above = source[0][part, at, PAD - 1 : PAD - 1 + span, :]
                    below = source[0][part, at, PAD + 1 : PAD + 1 + span, :]
                    here = source[1][part, at]
                    summed = here + jnp.where((slot + per - q) % per < 2, above, below)
                    parts.append(jnp.tanh(summed + b2_ref[0:1, :]) * valid)
                for t in range(per):
                    value = parts[0]
                    for q in range(1, per):
                        value = jnp.where(slot == (t + q) % per, parts[q], value)

                    def turned(by):
                        by = channels * (by - t) % LANES
                        return pltpu.roll(value, by, 1) if by else value

                    parity, pixel = t // 2, t % 2
                    column = 2 * xh + pixel
                    lines = slice(PAD, PAD + span)
                    t_ref[k, 4 + column, parity, side, half, lines, :] = turned(0)
                    n = 2 * side + half
                    step, edge, border = (1, 0, column - 4) if xh >= 2 else (-1, per - 1, 12 + column)
                    moved = turned(step)
                    own = t_ref.at[k, border, parity, side, half, lines, :]
                    if 0 <= n + step < 4:
                        other = t_ref.at[k, border, parity, (n + step) // 2, (n + step) % 2, lines, :]
                        pltpu.store(other, moved, mask=jnp.broadcast_to(slot == edge, moved.shape))
                    if 0 <= n - step < 4:
                        pltpu.store(own, moved, mask=jnp.broadcast_to(slot != edge, moved.shape))
                    else:
                        own[...] = jnp.where(slot == edge, 0.0, moved)

    def encode(k, carry):
        extra = REACH * (sections - k)
        section = jnp.where(k == 0, 0, chain_ref[jnp.maximum(k - 1, 0)])
        first = jnp.where(k == 0, 0, HALO + LATER * (section - 1))
        low = pl.ds(pl.multiple_of(first + jnp.where(k == 0, HALO - LATER, 0), 8), LATER)
        high = pl.ds(pl.multiple_of(first, 8), LATER)
        base = pl.multiple_of(2 * extra + HALO, 8)
        for half in range(2):
            cols = slice(LANES * half, LANES * (half + 1))
            z_ref[half, pl.ds(base - LATER, LATER), :] = lo_ref[low, cols].astype(jnp.float32)
            z_ref[half, pl.ds(base, 2 * rows), :] = img_ref[section, :, cols].astype(jnp.float32)
            z_ref[half, pl.ds(base + 2 * rows, LATER), :] = hi_ref[high, cols].astype(jnp.float32)

        @pl.when(k == 0)
        def _():
            for half in range(2):
                cols = slice(LANES * half, LANES * (half + 1))
                far = HALO - LATER
                z_ref[half, pl.ds(base - HALO, far), :] = lo_ref[0:far, cols].astype(jnp.float32)
                z_ref[half, pl.ds(base + 2 * rows + LATER, far), :] = hi_ref[LATER:HALO, cols].astype(jnp.float32)

        valid = inside_mask(k)
        for group in range(groups):
            side, place = divmod(group, groups // 2)
            at = group // 2 + groups // 2 * (group % 2)
            pieces = []
            for row in range(5):
                here = z_ref[side, pl.ds(HALO - 5 + row, span, stride=4), :]
                if place == 0 or (place == groups // 2 - 1 and side == 0):
                    if side == 0 and place == 0:
                        here = jnp.where(lane < LANES // 2, here, 0.0)
                    else:
                        other = z_ref[1 - side, pl.ds(HALO - 5 + row, span, stride=4), :]
                        low, high = (here, other) if side == 1 else (other, here)
                        here = jnp.where(lane < LANES // 2, low, high)
                start = PITCH * (row % 3)
                shift = (start - (2 * LANES // groups * place - 3)) % LANES
                pieces.append(pltpu.roll(here.astype(jnp.bfloat16), shift, 1))
            left = jnp.where(lane < PITCH, pieces[0], jnp.where(lane < 2 * PITCH, pieces[1], pieces[2]))
            right = jnp.where(lane < PITCH, pieces[3], jnp.where(lane < BIAS_LANE - LANES, pieces[4], valid.astype(jnp.bfloat16)))
            x_ref[pl.ds(span * at, span), 0:LANES] = left * valid.astype(jnp.bfloat16)
            x_ref[pl.ds(span * at, span), LANES:WIDE] = right * valid.astype(jnp.bfloat16)

        buffers = ((a0_ref, b0_ref), (a1_ref, b1_ref))
        for xh in range(4):
            layers(xh, buffers[xh % 2])
            features(k if xh else jnp.maximum(k - 1, 0), (xh - 1) % 4, buffers[(xh - 1) % 2])
        return carry

    lax.fori_loop(0, sections + 1, encode, 0)
    features(sections, 3, (a1_ref, b1_ref))

    scale = SHARPNESS / channels * math.log2(math.e)
    sub8 = lax.broadcasted_iota(jnp.int32, (8, LANES), 0)
    lane8 = lane_index((8, LANES))
    wide = lane_index((1, WIDE))
    x_of = (wide // 8) % 4
    y_of = 2 * (wide % 4) + (wide // 4) % 2
    row_at = 2 * lax.broadcasted_iota(jnp.int32, (2, 8, WIDE), 1) + lax.broadcasted_iota(jnp.int32, (2, 8, WIDE), 0)
    row_weight = row_at.astype(jnp.float32)
    row_mask = jnp.where((row_at >= y_of) & (row_at <= y_of + 2 * REACH), 1.0, 0.0)
    pick = channels * ((lane8 // 8) % 4) + 8 * (lane8 % 4) + 4 * (sub8 % 2) + sub8 // 2
    beyond = [jnp.where(x_of > m, 9.0, 0.0) for m in range(3)]
    patch = [jnp.where(slot == q, 1.0, 0.0).astype(jnp.bfloat16) for q in range(per)]

    def gather(values, index):
        return jnp.take_along_axis(values, index, axis=1, mode="promise_in_bounds")

    starts = [0]
    for k in range(1, sections + 1):
        starts.append(starts[-1] + pl.cdiv(rows + 2 * REACH * (sections - k), 16))
    blocks = starts[-1]

    def place(t):
        t = jnp.clip(t, 0, blocks - 1)
        k, first = 1, 0
        for n in range(1, sections):
            k = k + jnp.where(t >= starts[n], 1, 0)
            first = jnp.where(t >= starts[n], starts[n], first)
        return k, 2 * (t - first)

    def scores(k, i, side):
        lhs, rhs = [], [[], []]
        for half in range(2):
            window = t_ref[k - 1, :, :, side, half, pl.ds(PAD + 1 + 4 * i, 8), :]
            lhs.append(window.reshape(16 * 16, LANES).astype(jnp.bfloat16))
            even = t_ref[k, 4:12, 0, side, half, pl.ds(PAD + 1 + 4 * i, 8), :]
            odd = t_ref[k, 4:12, 1, side, half, pl.ds(PAD - 3 + 4 * i, 8), :]
            current = jnp.where(sub8 < 4, even, odd) * scale
            current = current.reshape(64, LANES).astype(jnp.bfloat16)
            for h in range(2):
                mine = current[32 * h : 32 * (h + 1)]
                nothing = jnp.zeros_like(mine)
                for q in range(per):
                    masked = mine * patch[q]
                    rhs[h].append(jnp.concatenate([masked, nothing] if half == 0 else [nothing, masked], axis=1))
        lhs = jnp.concatenate(lhs, axis=1)
        return [
            lax.dot_general(
                lhs[64 * h : 64 * h + 192], jnp.concatenate(rhs[h], axis=0), (((1,), (1,)), ((), ())),
                preferred_element_type=jnp.float32,
            )
            for h in range(2)
        ]

    def means(source, at):
        for m in range(8, -1, -1):
            score = source[at, 16 * m : 16 * m + 16, :]
            if m < 3:
                score = jnp.where(x_of <= m, score, source[at, 16 * m + 144 : 16 * m + 160, :])
            term = jnp.exp2(score).reshape(2, 8, WIDE)
            running = running + term if m < 8 else term
            if m:
                moment = moment + running if m < 8 else running
            if m < 3:
                moment = moment + term * beyond[m]
        running = running * row_mask
        moment = moment * row_mask
        total = jnp.sum(running[0] + running[1], axis=0, keepdims=True)
        moved = running * row_weight
        y_sum = jnp.sum(moved[0] + moved[1], axis=0, keepdims=True)
        x_sum = jnp.sum(moment[0] + moment[1], axis=0, keepdims=True)
        return y_sum / total, x_sum / total

    def compose(k, i, down, across):
        extra = REACH * (sections - k)
        whole = jnp.floor(across)
        part = across - whole
        left = lane8 + whole.astype(jnp.int32)
        right = left + 1
        left_weight = jnp.where((left >= 0) & (left < LANES), 1.0 - part, 0.0)
        right_weight = jnp.where((right >= 0) & (right < LANES), part, 0.0)
        left = jnp.clip(left, 0, LANES - 1)
        right = jnp.clip(right, 0, LANES - 1)
        sums = [down, across]
        shift = jnp.where(k == 1, FIELD_HALO - REACH * sections, 0)
        for step in range(-REACH, REACH + 1):
            row_part = jnp.maximum(0.0, 1.0 - jnp.abs(down - step))
            for c in range(2):
                values = f_ref[k - 1, c, pl.ds(8 * i + REACH + step + shift, 8), :]
                mixed = left_weight * gather(values, left) + right_weight * gather(values, right)
                sums[c] = sums[c] + row_part * mixed
        row = sub8 + 8 * i - extra + tile * rows
        inside = (row >= 0) & (row < total_rows)
        return [jnp.where(inside, value, 0.0) for value in sums]

    def fill(t, target, n, side):
        k, i = place(t)
        target[4 * n + 2 * side], target[4 * n + 2 * side + 1] = scores(k, i + n, side)

    def finish(t, found):
        k, i = place(t)
        fields = [compose(k, i + n, found[2 * n], found[2 * n + 1]) for n in range(2)]
        for n in range(2):
            for c in range(2):
                f_ref[k, c, pl.ds(pl.multiple_of(8 * i + 8 * n, 8), 8), :] = fields[n][c]

    def step(t, carry, source, target):
        found = []
        for n in range(2):
            down = jnp.zeros((8, LANES), jnp.float32)
            across = jnp.zeros((8, LANES), jnp.float32)
            for side in range(2):
                fill(t + 1, target, n, side)
                for h in range(2):
                    at = 4 * n + 2 * side + h
                    y_mean, x_mean = means(source, at)
                    for half in range(2):
                        keep = (lane8 // 64 == side) & ((lane8 // 32) % 2 == half) & ((lane8 // 4) % 2 == h)
                        cols = slice(LANES * half, LANES * (half + 1))
                        down = jnp.where(keep, gather(jnp.broadcast_to(y_mean[:, cols], (8, LANES)), pick), down)
                        across = jnp.where(keep, gather(jnp.broadcast_to(x_mean[:, cols], (8, LANES)), pick), across)
            found.append(down - (REACH + sub8).astype(jnp.float32))
            found.append(across - (REACH + lane8 % 4).astype(jnp.float32))
        finish(t - 1, carry)
        return tuple(found)

    def two_steps(j, carry):
        carry = step(2 * j, carry, s0_ref, s1_ref)
        return step(2 * j + 1, carry, s1_ref, s0_ref)

    for at in range(4):
        fill(0, s0_ref, at // 2, at % 2)
    turns = pl.cdiv(blocks, 2)
    found = lax.fori_loop(0, turns, two_steps, (jnp.zeros((8, LANES), jnp.float32),) * 4)
    finish(2 * turns - 1, found)
    for k in range(1, sections + 1):
        extra = REACH * (sections - k)
        out_ref[k - 1] = f_ref[k, :, extra : extra + rows, :]


def on_device(images, section_order, prev_field, conv1_weight, conv1_bias, conv2_weight, conv2_bias):
    count = lax.axis_size("tile")
    forward = [(i, i + 1) for i in range(count - 1)]
    backward = [(target, source) for source, target in forward]
    pixel_rows, columns = images.shape[1:]
    sections = section_order.shape[0]
    rows = prev_field.shape[1]
    channels = conv1_weight.shape[0]

    vmem = pl.BlockSpec(memory_space=pltpu.VMEM)
    hbm = pl.BlockSpec(memory_space=pl.ANY)
    held = HALO + LATER * sections + FIELD_HALO
    up, down = pl.pallas_call(
        pack,
        out_shape=(jax.ShapeDtypeStruct((held, columns), images.dtype),) * 2,
        in_specs=[hbm, hbm],
        out_specs=(vmem, vmem),
        scratch_shapes=[
            pltpu.VMEM((2, 2, FIELD_HALO, prev_field.shape[2]), jnp.float32),
            pltpu.SemaphoreType.DMA((2, sections + 2)),
        ],
        compiler_params=pltpu.CompilerParams(vmem_limit_bytes=66850000),
        name="pack",
    )(images, prev_field)
    chain = section_order + 1
    lo = lax.ppermute(up, "tile", forward)
    hi = lax.ppermute(down, "tile", backward)

    w1, w2, b2 = pl.pallas_call(
        prepare,
        out_shape=(
            jax.ShapeDtypeStruct((WINDOWS, WIDE, WIDE), jnp.bfloat16),
            jax.ShapeDtypeStruct((LANES // channels, WIDE, WIDE), jnp.bfloat16),
            jax.ShapeDtypeStruct((8, LANES), jnp.float32),
        ),
        in_specs=[pl.BlockSpec(memory_space=pltpu.SMEM)] + [vmem] * 5,
        out_specs=(vmem,) * 3,
        cost_estimate=pl.CostEstimate(flops=10**9, bytes_accessed=10**6, transcendentals=0),
        compiler_params=pltpu.CompilerParams(vmem_limit_bytes=12 * 1024 * 1024),
        name="weights",
    )(chain, jnp.asarray(first_layer_lanes()), conv1_weight, conv1_bias[None], conv2_weight, conv2_bias[None])

    groups = columns // (4 * WINDOWS)
    span = (rows + 2 * REACH * sections) // 2 + 4
    return pl.pallas_call(
        functools.partial(kernel, sections, rows, rows * count, channels),
        out_shape=jax.ShapeDtypeStruct((sections, 2, rows, prev_field.shape[2]), jnp.float32),
        in_specs=[pl.BlockSpec(memory_space=pltpu.SMEM)] + [vmem] * 7,
        out_specs=vmem,
        scratch_shapes=[
            pltpu.VMEM((2, 2 * rows + 96, LANES), jnp.float32),
            pltpu.VMEM((groups * span, WIDE), jnp.bfloat16),
            pltpu.VMEM((2, groups, span + 2 * PAD, LANES), jnp.float32),
            pltpu.VMEM((2, groups, span + 2 * PAD, LANES), jnp.float32),
            pltpu.VMEM((2, groups, span, LANES), jnp.float32),
            pltpu.VMEM((2, groups, span, LANES), jnp.float32),
            pltpu.VMEM((sections + 1, 16, 2, 2, 2, span + 2 * PAD, LANES), jnp.float32),
            pltpu.VMEM((sections + 1, 2, rows + 2 * FIELD_HALO + 8, LANES), jnp.float32),
            pltpu.VMEM((8, 192, WIDE), jnp.float32),
            pltpu.VMEM((8, 192, WIDE), jnp.float32),
        ],
        compiler_params=pltpu.CompilerParams(vmem_limit_bytes=44 * 1024 * 1024),
        name="align",
    )(chain, images, lo, hi, prev_field, w1, w2, b2)


def solution(mesh):
    in_specs = (P("parts", "tile", None), P("parts"), P("parts", "tile", None), P(), P(), P(), P())
    out_specs = P("parts", None, "tile", None)
    return jax.shard_map(on_device, mesh=mesh, in_specs=in_specs, out_specs=out_specs, check_vma=False)
```

```python
import functools
import math

import jax
import jax.numpy as jnp
import numpy as np
from jax import lax
from jax.experimental import pallas as pl
from jax.experimental.pallas import tpu as pltpu
from jax.sharding import PartitionSpec as P

SHARPNESS = 16.0
REACH = 4
LANES = 128
WIDE = 256
HALO = 32
LATER = 24
FIELD_HALO = 16
PITCH = 40
BIAS_LANE = 248
PAD = 8
WINDOWS = 8


def first_layer_lanes():
    lanes = np.full((1, LANES), -WIDE, np.int32)
    for slot in range(8):
        for tap in range(9):
            pixel_row = 2 * (slot // 4) + tap // 3
            start = PITCH * pixel_row if pixel_row < 3 else LANES + PITCH * (pixel_row - 3)
            lanes[0, 9 * slot + tap] = start + 2 * (slot % 4) + tap % 3
    return lanes


def pack(img_ref, fld_ref, up_ref, down_ref, field_ref, sem):
    sections = img_ref.shape[0] - 1
    copies = []
    for side, out_ref in enumerate((up_ref, down_ref)):
        at = 0
        for section in range(sections + 1):
            count = LATER if section else HALO
            first = 0 if side else img_ref.shape[1] - count
            copies.append(
                pltpu.make_async_copy(
                    img_ref.at[section, first : first + count], out_ref.at[at : at + count], sem.at[side, section]
                )
            )
            at += count
        first = 0 if side else fld_ref.shape[1] - FIELD_HALO
        copies.append(
            pltpu.make_async_copy(
                fld_ref.at[:, first : first + FIELD_HALO], field_ref.at[side], sem.at[side, sections + 1]
            )
        )
    for copy in copies:
        copy.start()
    for copy in copies:
        copy.wait()
    for side, out_ref in enumerate((up_ref, down_ref)):
        field = jnp.concatenate([field_ref[side, 0], field_ref[side, 1]], axis=1)
        out_ref[HALO + LATER * sections :, :] = field.astype(jnp.bfloat16)


def prepare(chain_ref, lanes_ref, c1_ref, b1_ref, c2_ref, b2_ref, w1_ref, w2_ref, bias_ref):
    del chain_ref
    channels, taps = c1_ref.shape

    def indices(shape):
        return [lax.broadcasted_iota(jnp.int32, shape, axis) for axis in range(2)]

    def ones_where(condition):
        return jnp.where(condition, 1.0, 0.0).astype(jnp.bfloat16)

    def repeated(values, dims):
        return lax.dot_general(values, spread, (dims, ((), ())), preferred_element_type=jnp.float32)

    row, col = indices((channels, WIDE))
    spread = ones_where(col % channels == row)

    def pieces(ref):
        rest = jnp.broadcast_to(ref[...], (8, channels))
        row = lax.broadcasted_iota(jnp.int32, (8, channels), 0)
        total = jnp.zeros((8, channels), jnp.float32)
        for n in range(3):
            top = rest.astype(jnp.bfloat16).astype(jnp.float32)
            total = jnp.where(row == n, top, total)
            rest = rest - top
        return repeated(total.astype(jnp.bfloat16), ((1,), (0,)))

    bias_ref[...] = jnp.broadcast_to(jnp.sum(pieces(b2_ref), axis=0, keepdims=True), (8, WIDE))[:, :LANES]

    by_tap = repeated(c1_ref[...], ((0,), (0,)))
    row, col = indices((LANES, WIDE))
    table = jnp.zeros((LANES, WIDE), jnp.float32)
    slot = col // channels
    for tap in range(taps):
        table = jnp.where(row == taps * slot + tap, by_tap[tap : tap + 1], table)
    bias = pieces(b1_ref)
    for n in range(3):
        table = jnp.where(row == 8 * taps + n, bias[n : n + 1], table)
    table = table.astype(jnp.bfloat16)
    row, col = indices((WIDE, LANES))
    bias_lane = (col >= 8 * taps) & (col < 8 * taps + 3) & (row == BIAS_LANE + col - 8 * taps)
    for window in range(WINDOWS):
        pick = ones_where((row == lanes_ref[...] + 4 * window) | bias_lane)
        w1_ref[window] = jnp.dot(pick, table, preferred_element_type=jnp.float32).astype(jnp.bfloat16)

    row, col = indices((WIDE, WIDE))
    slot_in, slot_out = row // channels, col // channels
    row_out = slot_out // 2
    row_out = jnp.where(row_out == 0, 2, row_out - 2)
    row_step = slot_in // 4 - row_out
    col_step = slot_in % 4 - 1 - slot_out % 2
    near = (jnp.abs(row_step) <= 1) & (jnp.abs(col_step) <= 1)
    tap_at = jnp.where(near, 3 * row_step + col_step + 4, -1)
    table = jnp.zeros((WIDE, WIDE), jnp.float32)
    for tap in range(taps):
        block = repeated(c2_ref[tap], ((0,), (0,)))
        table = jnp.where(tap_at == tap, jnp.concatenate([block] * (WIDE // channels), axis=0), table)
    table = table.astype(jnp.bfloat16)
    for skew in range(LANES // channels):
        for half in range(2):
            cols = slice(LANES * half, LANES * (half + 1))
            part = table[:, cols]
            w2_ref[skew, :, cols] = pltpu.roll(part, channels * skew, 1) if skew else part


def lane_index(shape):
    return lax.broadcasted_iota(jnp.int32, shape, len(shape) - 1)


def kernel(
    sections, rows, total_rows, channels,
    chain_ref, img_ref, lo_ref, hi_ref, fld_ref, w1_ref, w2_ref, b2_ref,
    out_ref, z_ref, x_ref, a0_ref, a1_ref, b0_ref, b1_ref, t_ref, f_ref, s0_ref, s1_ref,
):
    groups = a0_ref.shape[1]
    largest = x_ref.shape[0] // groups
    per = LANES // channels
    lane = lane_index((1, LANES))
    slot = lane // channels
    tile = lax.axis_index("tile")
    pairs_total = total_rows // 2

    z_ref[...] = jnp.zeros_like(z_ref)
    pictures = HALO + LATER * sections
    f_ref[0, :, FIELD_HALO : FIELD_HALO + rows, :] = fld_ref[...]
    for ref, start in ((lo_ref, 0), (hi_ref, FIELD_HALO + rows)):
        for c in range(2):
            part = ref[pictures : pictures + FIELD_HALO, LANES * c : LANES * (c + 1)]
            f_ref[0, c, start : start + FIELD_HALO, :] = part.astype(jnp.float32)

    def inside_mask(k, span):
        pair = lax.broadcasted_iota(jnp.int32, (span, LANES), 0) + tile * (rows // 2) - 1
        pair = pair - REACH * (sections - k) // 2
        return jnp.where((pair >= 0) & (pair < pairs_total), 1.0, 0.0)

    def layers(xh, target, span):
        for part in range(2):
            first = jnp.dot(x_ref[: groups * span], w1_ref[xh + 4 * part], preferred_element_type=jnp.float32)
            first = jnp.maximum(first, 0.0)
            edge = (lane_index((1, WIDE)) // channels) % 4
            if xh == 0 and part == 0:
                first = jnp.concatenate([jnp.where(edge == 0, 0.0, first[:span]), first[span:]], axis=0)
            if xh == 3 and part == 1:
                first = jnp.concatenate([first[:-span], jnp.where(edge == 3, 0.0, first[-span:])], axis=0)
            first = first.astype(jnp.bfloat16)
            for odd in range(2):
                half = groups * span // 2
                second = jnp.dot(
                    first[half * odd : half * (odd + 1)], w2_ref[part + 2 * odd], preferred_element_type=jnp.float32
                )
                at = groups // 2 * odd
                second = second.reshape(groups // 2, span, WIDE)
                target[0][part, at : at + groups // 2, PAD : PAD + span, :] = second[:, :, :LANES]
                target[1][part, at : at + groups // 2, 0:span, :] = second[:, :, LANES:]

    def features(k, xh, source, span):
        valid = inside_mask(k, span)
        for side in range(2):
            for half in range(2):
                parts = []
                for q in range(per):
                    part, odd = q % 2, q // 2
                    at = 2 * side + half + 4 * odd
                    above = source[0][part, at, PAD - 1 : PAD - 1 + span, :]
                    below = source[0][part, at, PAD + 1 : PAD + 1 + span, :]
                    here = source[1][part, at, 0:span, :]
                    summed = here + jnp.where((slot + per - q) % per < 2, above, below)
                    parts.append(jnp.tanh(summed + b2_ref[0:1, :]) * valid)
                for t in range(per):
                    value = parts[0]
                    for q in range(1, per):
                        value = jnp.where(slot == (t + q) % per, parts[q], value)

                    def turned(by):
                        by = channels * (by - t) % LANES
                        return pltpu.roll(value, by, 1) if by else value

                    parity, pixel = t // 2, t % 2
                    column = 2 * xh + pixel
                    lines = slice(PAD, PAD + span)
                    t_ref[k, 4 + column, parity, side, half, lines, :] = turned(0)
                    n = 2 * side + half
                    step, edge, border = (1, 0, column - 4) if xh >= 2 else (-1, per - 1, 12 + column)
                    moved = turned(step)
                    own = t_ref.at[k, border, parity, side, half, lines, :]
                    if 0 <= n + step < 4:
                        other = t_ref.at[k, border, parity, (n + step) // 2, (n + step) % 2, lines, :]
                        pltpu.store(other, moved, mask=jnp.broadcast_to(slot == edge, moved.shape))
                    if 0 <= n - step < 4:
                        pltpu.store(own, moved, mask=jnp.broadcast_to(slot != edge, moved.shape))
                    else:
                        own[...] = jnp.where(slot == edge, 0.0, moved)

    def encode(span, before, k, carry):
        extra = REACH * (sections - k)
        section = jnp.where(k == 0, 0, chain_ref[jnp.maximum(k - 1, 0)])
        first = jnp.where(k == 0, 0, HALO + LATER * (section - 1))
        low = pl.ds(pl.multiple_of(first + jnp.where(k == 0, HALO - LATER, 0), 8), LATER)
        high = pl.ds(pl.multiple_of(first, 8), LATER)
        base = pl.multiple_of(2 * extra + HALO, 8)
        for half in range(2):
            cols = slice(LANES * half, LANES * (half + 1))
            z_ref[half, pl.ds(base - LATER, LATER), :] = lo_ref[low, cols].astype(jnp.float32)
            z_ref[half, pl.ds(base, 2 * rows), :] = img_ref[section, :, cols].astype(jnp.float32)
            z_ref[half, pl.ds(base + 2 * rows, LATER), :] = hi_ref[high, cols].astype(jnp.float32)

        @pl.when(k == 0)
        def _():
            for half in range(2):
                cols = slice(LANES * half, LANES * (half + 1))
                far = HALO - LATER
                z_ref[half, pl.ds(base - HALO, far), :] = lo_ref[0:far, cols].astype(jnp.float32)
                z_ref[half, pl.ds(base + 2 * rows + LATER, far), :] = hi_ref[LATER:HALO, cols].astype(jnp.float32)

        valid = inside_mask(k, span)
        for group in range(groups):
            side, place = divmod(group, groups // 2)
            at = group // 2 + groups // 2 * (group % 2)
            pieces = []
            for row in range(5):
                here = z_ref[side, pl.ds(HALO - 5 + row, span, stride=4), :]
                if place == 0 or (place == groups // 2 - 1 and side == 0):
                    if side == 0 and place == 0:
                        here = jnp.where(lane < LANES // 2, here, 0.0)
                    else:
                        other = z_ref[1 - side, pl.ds(HALO - 5 + row, span, stride=4), :]
                        low, high = (here, other) if side == 1 else (other, here)
                        here = jnp.where(lane < LANES // 2, low, high)
                start = PITCH * (row % 3)
                shift = (start - (2 * LANES // groups * place - 3)) % LANES
                pieces.append(pltpu.roll(here.astype(jnp.bfloat16), shift, 1))
            left = jnp.where(lane < PITCH, pieces[0], jnp.where(lane < 2 * PITCH, pieces[1], pieces[2]))
            right = jnp.where(lane < PITCH, pieces[3], jnp.where(lane < BIAS_LANE - LANES, pieces[4], valid.astype(jnp.bfloat16)))
            x_ref[pl.ds(span * at, span), 0:LANES] = left * valid.astype(jnp.bfloat16)
            x_ref[pl.ds(span * at, span), LANES:WIDE] = right * valid.astype(jnp.bfloat16)

        buffers = ((a0_ref, b0_ref), (a1_ref, b1_ref))
        for xh in range(4):
            layers(xh, buffers[xh % 2], span)
            last = buffers[(xh - 1) % 2]
            if xh:
                features(k, xh - 1, last, span)
            else:
                features(jnp.maximum(k - 1, 0), 3, last, before)
        return carry

    half = (sections + 1) // 2
    fewer = pl.cdiv((rows + 2 * REACH * (sections - half)) // 2 + 2, 8) * 8
    lax.fori_loop(0, half, functools.partial(encode, largest, largest), 0)
    encode(fewer, largest, half, 0)
    lax.fori_loop(half + 1, sections + 1, functools.partial(encode, fewer, fewer), 0)
    features(sections, 3, (a1_ref, b1_ref), fewer)

    scale = SHARPNESS / channels * math.log2(math.e)
    sub8 = lax.broadcasted_iota(jnp.int32, (8, LANES), 0)
    lane8 = lane_index((8, LANES))
    wide = lane_index((1, WIDE))
    x_of = (wide // 8) % 4
    y_of = 2 * (wide % 4) + (wide // 4) % 2
    row_at = 2 * lax.broadcasted_iota(jnp.int32, (2, 8, WIDE), 1) + lax.broadcasted_iota(jnp.int32, (2, 8, WIDE), 0)
    row_weight = row_at.astype(jnp.float32)
    row_mask = jnp.where((row_at >= y_of) & (row_at <= y_of + 2 * REACH), 1.0, 0.0)
    pick = channels * ((lane8 // 8) % 4) + 8 * (lane8 % 4) + 4 * (sub8 % 2) + sub8 // 2
    beyond = [jnp.where(x_of > m, 9.0, 0.0) for m in range(3)]
    patch = [jnp.where(slot == q, 1.0, 0.0).astype(jnp.bfloat16) for q in range(per)]

    def gather(values, index):
        return jnp.take_along_axis(values, index, axis=1, mode="promise_in_bounds")

    starts = [0]
    for k in range(1, sections + 1):
        starts.append(starts[-1] + pl.cdiv(rows + 2 * REACH * (sections - k), 16))
    blocks = starts[-1]

    def place(t):
        t = jnp.clip(t, 0, blocks - 1)
        k, first = 1, 0
        for n in range(1, sections):
            k = k + jnp.where(t >= starts[n], 1, 0)
            first = jnp.where(t >= starts[n], starts[n], first)
        return k, 2 * (t - first)

    def scores(k, i, side):
        lhs, rhs = [], [[], []]
        for half in range(2):
            window = t_ref[k - 1, :, :, side, half, pl.ds(PAD + 1 + 4 * i, 8), :]
            lhs.append(window.reshape(16 * 16, LANES).astype(jnp.bfloat16))
            even = t_ref[k, 4:12, 0, side, half, pl.ds(PAD + 1 + 4 * i, 8), :]
            odd = t_ref[k, 4:12, 1, side, half, pl.ds(PAD - 3 + 4 * i, 8), :]
            current = jnp.where(sub8 < 4, even, odd) * scale
            current = current.reshape(64, LANES).astype(jnp.bfloat16)
            for h in range(2):
                mine = current[32 * h : 32 * (h + 1)]
                nothing = jnp.zeros_like(mine)
                for q in range(per):
                    masked = mine * patch[q]
                    rhs[h].append(jnp.concatenate([masked, nothing] if half == 0 else [nothing, masked], axis=1))
        lhs = jnp.concatenate(lhs, axis=1)
        return [
            lax.dot_general(
                lhs[64 * h : 64 * h + 192], jnp.concatenate(rhs[h], axis=0), (((1,), (1,)), ((), ())),
                preferred_element_type=jnp.float32,
            )
            for h in range(2)
        ]

    def means(source, at):
        for m in range(8, -1, -1):
            score = source[at, 16 * m : 16 * m + 16, :]
            if m < 3:
                score = jnp.where(x_of <= m, score, source[at, 16 * m + 144 : 16 * m + 160, :])
            term = jnp.exp2(score).reshape(2, 8, WIDE)
            running = running + term if m < 8 else term
            if m:
                moment = moment + running if m < 8 else running
            if m < 3:
                moment = moment + term * beyond[m]
        running = running * row_mask
        moment = moment * row_mask
        total = jnp.sum(running[0] + running[1], axis=0, keepdims=True)
        moved = running * row_weight
        y_sum = jnp.sum(moved[0] + moved[1], axis=0, keepdims=True)
        x_sum = jnp.sum(moment[0] + moment[1], axis=0, keepdims=True)
        return y_sum / total, x_sum / total

    def compose(k, i, down, across):
        extra = REACH * (sections - k)
        whole = jnp.floor(across)
        part = across - whole
        left = lane8 + whole.astype(jnp.int32)
        right = left + 1
        left_weight = jnp.where((left >= 0) & (left < LANES), 1.0 - part, 0.0)
        right_weight = jnp.where((right >= 0) & (right < LANES), part, 0.0)
        left = jnp.clip(left, 0, LANES - 1)
        right = jnp.clip(right, 0, LANES - 1)
        sums = [down, across]
        shift = jnp.where(k == 1, FIELD_HALO - REACH * sections, 0)
        for step in range(-REACH, REACH + 1):
            row_part = jnp.maximum(0.0, 1.0 - jnp.abs(down - step))
            for c in range(2):
                values = f_ref[k - 1, c, pl.ds(8 * i + REACH + step + shift, 8), :]
                mixed = left_weight * gather(values, left) + right_weight * gather(values, right)
                sums[c] = sums[c] + row_part * mixed
        row = sub8 + 8 * i - extra + tile * rows
        inside = (row >= 0) & (row < total_rows)
        return [jnp.where(inside, value, 0.0) for value in sums]

    def fill(t, target, n, side):
        k, i = place(t)
        target[4 * n + 2 * side], target[4 * n + 2 * side + 1] = scores(k, i + n, side)

    def finish(t, found):
        k, i = place(t)
        fields = [compose(k, i + n, found[2 * n], found[2 * n + 1]) for n in range(2)]
        for n in range(2):
            for c in range(2):
                f_ref[k, c, pl.ds(pl.multiple_of(8 * i + 8 * n, 8), 8), :] = fields[n][c]

    def step(t, carry, source, target):
        found = []
        for n in range(2):
            down = jnp.zeros((8, LANES), jnp.float32)
            across = jnp.zeros((8, LANES), jnp.float32)
            for side in range(2):
                fill(t + 1, target, n, side)
                for h in range(2):
                    at = 4 * n + 2 * side + h
                    y_mean, x_mean = means(source, at)
                    for half in range(2):
                        keep = (lane8 // 64 == side) & ((lane8 // 32) % 2 == half) & ((lane8 // 4) % 2 == h)
                        cols = slice(LANES * half, LANES * (half + 1))
                        down = jnp.where(keep, gather(jnp.broadcast_to(y_mean[:, cols], (8, LANES)), pick), down)
                        across = jnp.where(keep, gather(jnp.broadcast_to(x_mean[:, cols], (8, LANES)), pick), across)
            found.append(down - (REACH + sub8).astype(jnp.float32))
            found.append(across - (REACH + lane8 % 4).astype(jnp.float32))
        finish(t - 1, carry)
        return tuple(found)

    def two_steps(j, carry):
        carry = step(2 * j, carry, s0_ref, s1_ref)
        return step(2 * j + 1, carry, s1_ref, s0_ref)

    for at in range(4):
        fill(0, s0_ref, at // 2, at % 2)
    turns = pl.cdiv(blocks, 2)
    found = lax.fori_loop(0, turns, two_steps, (jnp.zeros((8, LANES), jnp.float32),) * 4)
    finish(2 * turns - 1, found)
    for k in range(1, sections + 1):
        extra = REACH * (sections - k)
        out_ref[k - 1] = f_ref[k, :, extra : extra + rows, :]


def on_device(images, section_order, prev_field, conv1_weight, conv1_bias, conv2_weight, conv2_bias):
    count = lax.axis_size("tile")
    forward = [(i, i + 1) for i in range(count - 1)]
    backward = [(target, source) for source, target in forward]
    pixel_rows, columns = images.shape[1:]
    sections = section_order.shape[0]
    rows = prev_field.shape[1]
    channels = conv1_weight.shape[0]

    vmem = pl.BlockSpec(memory_space=pltpu.VMEM)
    hbm = pl.BlockSpec(memory_space=pl.ANY)
    held = HALO + LATER * sections + FIELD_HALO
    up, down = pl.pallas_call(
        pack,
        out_shape=(jax.ShapeDtypeStruct((held, columns), images.dtype),) * 2,
        in_specs=[hbm, hbm],
        out_specs=(vmem, vmem),
        scratch_shapes=[
            pltpu.VMEM((2, 2, FIELD_HALO, prev_field.shape[2]), jnp.float32),
            pltpu.SemaphoreType.DMA((2, sections + 2)),
        ],
        compiler_params=pltpu.CompilerParams(vmem_limit_bytes=66850000),
        name="pack",
    )(images, prev_field)
    chain = section_order + 1
    lo = lax.ppermute(up, "tile", forward)
    hi = lax.ppermute(down, "tile", backward)

    w1, w2, b2 = pl.pallas_call(
        prepare,
        out_shape=(
            jax.ShapeDtypeStruct((WINDOWS, WIDE, WIDE), jnp.bfloat16),
            jax.ShapeDtypeStruct((LANES // channels, WIDE, WIDE), jnp.bfloat16),
            jax.ShapeDtypeStruct((8, LANES), jnp.float32),
        ),
        in_specs=[pl.BlockSpec(memory_space=pltpu.SMEM)] + [vmem] * 5,
        out_specs=(vmem,) * 3,
        cost_estimate=pl.CostEstimate(flops=10**9, bytes_accessed=10**6, transcendentals=0),
        compiler_params=pltpu.CompilerParams(vmem_limit_bytes=12 * 1024 * 1024),
        name="weights",
    )(chain, jnp.asarray(first_layer_lanes()), conv1_weight, conv1_bias[None], conv2_weight, conv2_bias[None])

    groups = columns // (4 * WINDOWS)
    span = (rows + 2 * REACH * sections) // 2 + 4
    return pl.pallas_call(
        functools.partial(kernel, sections, rows, rows * count, channels),
        out_shape=jax.ShapeDtypeStruct((sections, 2, rows, prev_field.shape[2]), jnp.float32),
        in_specs=[pl.BlockSpec(memory_space=pltpu.SMEM)] + [vmem] * 7,
        out_specs=vmem,
        scratch_shapes=[
            pltpu.VMEM((2, 2 * rows + 96, LANES), jnp.float32),
            pltpu.VMEM((groups * span, WIDE), jnp.bfloat16),
            pltpu.VMEM((2, groups, span + 2 * PAD, LANES), jnp.float32),
            pltpu.VMEM((2, groups, span + 2 * PAD, LANES), jnp.float32),
            pltpu.VMEM((2, groups, span, LANES), jnp.float32),
            pltpu.VMEM((2, groups, span, LANES), jnp.float32),
            pltpu.VMEM((sections + 1, 16, 2, 2, 2, span + 2 * PAD, LANES), jnp.float32),
            pltpu.VMEM((sections + 1, 2, rows + 2 * FIELD_HALO + 8, LANES), jnp.float32),
            pltpu.VMEM((8, 192, WIDE), jnp.float32),
            pltpu.VMEM((8, 192, WIDE), jnp.float32),
        ],
        compiler_params=pltpu.CompilerParams(vmem_limit_bytes=44 * 1024 * 1024),
        name="align",
    )(chain, images, lo, hi, prev_field, w1, w2, b2)


def solution(mesh):
    in_specs = (P("parts", "tile", None), P("parts"), P("parts", "tile", None), P(), P(), P(), P())
    out_specs = P("parts", None, "tile", None)
    return jax.shard_map(on_device, mesh=mesh, in_specs=in_specs, out_specs=out_specs, check_vma=False)
```

```python
import functools
import math

import jax
import jax.numpy as jnp
import numpy as np
from jax import lax
from jax.experimental import pallas as pl
from jax.experimental.pallas import tpu as pltpu
from jax.sharding import PartitionSpec as P

SHARPNESS = 16.0
REACH = 4
LANES = 128
WIDE = 256
HALO = 32
LATER = 24
FIELD_HALO = 16
PITCH = 40
BIAS_LANE = 248
PAD = 8
WINDOWS = 8


def first_layer_lanes():
    lanes = np.full((1, LANES), -WIDE, np.int32)
    for slot in range(8):
        for tap in range(9):
            pixel_row = 2 * (slot // 4) + tap // 3
            start = PITCH * pixel_row if pixel_row < 3 else LANES + PITCH * (pixel_row - 3)
            lanes[0, 9 * slot + tap] = start + 2 * (slot % 4) + tap % 3
    return lanes


def pack(img_ref, fld_ref, up_ref, down_ref, field_ref, sem):
    sections = img_ref.shape[0] - 1
    copies = []
    for side, out_ref in enumerate((up_ref, down_ref)):
        at = 0
        for section in range(sections + 1):
            count = LATER if section else HALO
            first = 0 if side else img_ref.shape[1] - count
            copies.append(
                pltpu.make_async_copy(
                    img_ref.at[section, first : first + count], out_ref.at[at : at + count], sem.at[side, section]
                )
            )
            at += count
        first = 0 if side else fld_ref.shape[1] - FIELD_HALO
        copies.append(
            pltpu.make_async_copy(
                fld_ref.at[:, first : first + FIELD_HALO], field_ref.at[side], sem.at[side, sections + 1]
            )
        )
    for copy in copies:
        copy.start()
    for copy in copies:
        copy.wait()
    for side, out_ref in enumerate((up_ref, down_ref)):
        field = jnp.concatenate([field_ref[side, 0], field_ref[side, 1]], axis=1)
        out_ref[HALO + LATER * sections :, :] = field.astype(jnp.bfloat16)


def prepare(chain_ref, lanes_ref, c1_ref, b1_ref, c2_ref, b2_ref, w1_ref, w2_ref, bias_ref):
    del chain_ref
    channels, taps = c1_ref.shape

    def indices(shape):
        return [lax.broadcasted_iota(jnp.int32, shape, axis) for axis in range(2)]

    def ones_where(condition):
        return jnp.where(condition, 1.0, 0.0).astype(jnp.bfloat16)

    def repeated(values, dims):
        return lax.dot_general(values, spread, (dims, ((), ())), preferred_element_type=jnp.float32)

    row, col = indices((channels, WIDE))
    spread = ones_where(col % channels == row)

    def pieces(ref):
        rest = jnp.broadcast_to(ref[...], (8, channels))
        row = lax.broadcasted_iota(jnp.int32, (8, channels), 0)
        total = jnp.zeros((8, channels), jnp.float32)
        for n in range(3):
            top = rest.astype(jnp.bfloat16).astype(jnp.float32)
            total = jnp.where(row == n, top, total)
            rest = rest - top
        return repeated(total.astype(jnp.bfloat16), ((1,), (0,)))

    bias_ref[...] = jnp.broadcast_to(jnp.sum(pieces(b2_ref), axis=0, keepdims=True), (8, WIDE))[:, :LANES]

    by_tap = repeated(c1_ref[...], ((0,), (0,)))
    row, col = indices((LANES, WIDE))
    table = jnp.zeros((LANES, WIDE), jnp.float32)
    slot = col // channels
    for tap in range(taps):
        table = jnp.where(row == taps * slot + tap, by_tap[tap : tap + 1], table)
    bias = pieces(b1_ref)
    for n in range(3):
        table = jnp.where(row == 8 * taps + n, bias[n : n + 1], table)
    table = table.astype(jnp.bfloat16)
    row, col = indices((WIDE, LANES))
    bias_lane = (col >= 8 * taps) & (col < 8 * taps + 3) & (row == BIAS_LANE + col - 8 * taps)
    for window in range(WINDOWS):
        pick = ones_where((row == lanes_ref[...] + 4 * window) | bias_lane)
        w1_ref[window] = jnp.dot(pick, table, preferred_element_type=jnp.float32).astype(jnp.bfloat16)

    row, col = indices((WIDE, WIDE))
    slot_in, slot_out = row // channels, col // channels
    row_out = slot_out // 2
    row_out = jnp.where(row_out == 0, 2, row_out - 2)
    row_step = slot_in // 4 - row_out
    col_step = slot_in % 4 - 1 - slot_out % 2
    near = (jnp.abs(row_step) <= 1) & (jnp.abs(col_step) <= 1)
    tap_at = jnp.where(near, 3 * row_step + col_step + 4, -1)
    table = jnp.zeros((WIDE, WIDE), jnp.float32)
    for tap in range(taps):
        block = repeated(c2_ref[tap], ((0,), (0,)))
        table = jnp.where(tap_at == tap, jnp.concatenate([block] * (WIDE // channels), axis=0), table)
    table = table.astype(jnp.bfloat16)
    for skew in range(LANES // channels):
        for half in range(2):
            cols = slice(LANES * half, LANES * (half + 1))
            part = table[:, cols]
            w2_ref[skew, :, cols] = pltpu.roll(part, channels * skew, 1) if skew else part


def lane_index(shape):
    return lax.broadcasted_iota(jnp.int32, shape, len(shape) - 1)


def kernel(
    sections, rows, total_rows, channels,
    chain_ref, img_ref, lo_ref, hi_ref, fld_ref, w1_ref, w2_ref, b2_ref,
    out_ref, z_ref, x_ref, a0_ref, a1_ref, b0_ref, b1_ref, t_ref, f_ref, s0_ref, s1_ref,
):
    groups = a0_ref.shape[1]
    largest = x_ref.shape[0] // groups
    per = LANES // channels
    lane = lane_index((1, LANES))
    slot = lane // channels
    tile = lax.axis_index("tile")
    pairs_total = total_rows // 2

    z_ref[...] = jnp.zeros_like(z_ref)
    pictures = HALO + LATER * sections
    f_ref[0, :, FIELD_HALO : FIELD_HALO + rows, :] = fld_ref[...]
    for ref, start in ((lo_ref, 0), (hi_ref, FIELD_HALO + rows)):
        for c in range(2):
            part = ref[pictures : pictures + FIELD_HALO, LANES * c : LANES * (c + 1)]
            f_ref[0, c, start : start + FIELD_HALO, :] = part.astype(jnp.float32)

    def inside_mask(k, span):
        pair = lax.broadcasted_iota(jnp.int32, (span, LANES), 0) + tile * (rows // 2) - 1
        pair = pair - REACH * (sections - k) // 2
        return jnp.where((pair >= 0) & (pair < pairs_total), 1.0, 0.0)

    def layers(xh, target, span):
        for part in range(2):
            first = jnp.dot(x_ref[: groups * span], w1_ref[xh + 4 * part], preferred_element_type=jnp.float32)
            first = jnp.maximum(first, 0.0)
            edge = (lane_index((1, WIDE)) // channels) % 4
            if xh == 0 and part == 0:
                first = jnp.concatenate([jnp.where(edge == 0, 0.0, first[:span]), first[span:]], axis=0)
            if xh == 3 and part == 1:
                first = jnp.concatenate([first[:-span], jnp.where(edge == 3, 0.0, first[-span:])], axis=0)
            first = first.astype(jnp.bfloat16)
            for odd in range(2):
                half = groups * span // 2
                second = jnp.dot(
                    first[half * odd : half * (odd + 1)], w2_ref[part + 2 * odd], preferred_element_type=jnp.float32
                )
                at = groups // 2 * odd
                second = second.reshape(groups // 2, span, WIDE)
                target[0][part, at : at + groups // 2, PAD : PAD + span, :] = second[:, :, :LANES]
                target[1][part, at : at + groups // 2, 0:span, :] = second[:, :, LANES:]

    def features(k, xh, source, span):
        valid = inside_mask(k, span)
        for side in range(2):
            for half in range(2):
                parts = []
                for q in range(per):
                    part, odd = q % 2, q // 2
                    at = 2 * side + half + 4 * odd
                    above = source[0][part, at, PAD - 1 : PAD - 1 + span, :]
                    below = source[0][part, at, PAD + 1 : PAD + 1 + span, :]
                    here = source[1][part, at, 0:span, :]
                    summed = here + jnp.where((slot + per - q) % per < 2, above, below)
                    parts.append(jnp.tanh(summed + b2_ref[0:1, :]) * valid)
                for t in range(per):
                    value = parts[0]
                    for q in range(1, per):
                        value = jnp.where(slot == (t + q) % per, parts[q], value)

                    def turned(by):
                        by = channels * (by - t) % LANES
                        return pltpu.roll(value, by, 1) if by else value

                    parity, pixel = t // 2, t % 2
                    column = 2 * xh + pixel
                    lines = slice(PAD, PAD + span)
                    t_ref[k, 4 + column, parity, side, half, lines, :] = turned(0)
                    if isinstance(k, int) and k == sections:
                        continue
                    n = 2 * side + half
                    step, edge, border = (1, 0, column - 4) if xh >= 2 else (-1, per - 1, 12 + column)
                    moved = turned(step)
                    own = t_ref.at[k, border, parity, side, half, lines, :]
                    if 0 <= n + step < 4:
                        other = t_ref.at[k, border, parity, (n + step) // 2, (n + step) % 2, lines, :]
                        pltpu.store(other, moved, mask=jnp.broadcast_to(slot == edge, moved.shape))
                    if 0 <= n - step < 4:
                        pltpu.store(own, moved, mask=jnp.broadcast_to(slot != edge, moved.shape))
                    else:
                        own[...] = jnp.where(slot == edge, 0.0, moved)

    def encode(span, before, k, carry):
        extra = REACH * (sections - k)
        section = jnp.where(k == 0, 0, chain_ref[jnp.maximum(k - 1, 0)])
        first = jnp.where(k == 0, 0, HALO + LATER * (section - 1))
        low = pl.ds(pl.multiple_of(first + jnp.where(k == 0, HALO - LATER, 0), 8), LATER)
        high = pl.ds(pl.multiple_of(first, 8), LATER)
        base = pl.multiple_of(2 * extra + HALO, 8)
        for half in range(2):
            cols = slice(LANES * half, LANES * (half + 1))
            z_ref[half, pl.ds(base - LATER, LATER), :] = lo_ref[low, cols].astype(jnp.float32)
            z_ref[half, pl.ds(base, 2 * rows), :] = img_ref[section, :, cols].astype(jnp.float32)
            z_ref[half, pl.ds(base + 2 * rows, LATER), :] = hi_ref[high, cols].astype(jnp.float32)

        @pl.when(k == 0)
        def _():
            for half in range(2):
                cols = slice(LANES * half, LANES * (half + 1))
                far = HALO - LATER
                z_ref[half, pl.ds(base - HALO, far), :] = lo_ref[0:far, cols].astype(jnp.float32)
                z_ref[half, pl.ds(base + 2 * rows + LATER, far), :] = hi_ref[LATER:HALO, cols].astype(jnp.float32)

        valid = inside_mask(k, span)
        for group in range(groups):
            side, place = divmod(group, groups // 2)
            at = group // 2 + groups // 2 * (group % 2)
            pieces = []
            for row in range(5):
                here = z_ref[side, pl.ds(HALO - 5 + row, span, stride=4), :]
                if place == 0 or (place == groups // 2 - 1 and side == 0):
                    if side == 0 and place == 0:
                        here = jnp.where(lane < LANES // 2, here, 0.0)
                    else:
                        other = z_ref[1 - side, pl.ds(HALO - 5 + row, span, stride=4), :]
                        low, high = (here, other) if side == 1 else (other, here)
                        here = jnp.where(lane < LANES // 2, low, high)
                start = PITCH * (row % 3)
                shift = (start - (2 * LANES // groups * place - 3)) % LANES
                pieces.append(pltpu.roll(here.astype(jnp.bfloat16), shift, 1))
            left = jnp.where(lane < PITCH, pieces[0], jnp.where(lane < 2 * PITCH, pieces[1], pieces[2]))
            right = jnp.where(lane < PITCH, pieces[3], jnp.where(lane < BIAS_LANE - LANES, pieces[4], valid.astype(jnp.bfloat16)))
            x_ref[pl.ds(span * at, span), 0:LANES] = left * valid.astype(jnp.bfloat16)
            x_ref[pl.ds(span * at, span), LANES:WIDE] = right * valid.astype(jnp.bfloat16)

        buffers = ((a0_ref, b0_ref), (a1_ref, b1_ref))
        for xh in range(4):
            layers(xh, buffers[xh % 2], span)
            last = buffers[(xh - 1) % 2]
            if xh:
                features(k, xh - 1, last, span)
            else:
                features(jnp.maximum(k - 1, 0), 3, last, before)
        return carry

    half = (sections + 1) // 2
    fewer = pl.cdiv((rows + 2 * REACH * (sections - half)) // 2 + 2, 8) * 8
    lax.fori_loop(0, half, functools.partial(encode, largest, largest), 0)
    encode(fewer, largest, half, 0)
    lax.fori_loop(half + 1, sections + 1, functools.partial(encode, fewer, fewer), 0)
    features(sections, 3, (a1_ref, b1_ref), fewer)

    scale = SHARPNESS / channels * math.log2(math.e)
    sub8 = lax.broadcasted_iota(jnp.int32, (8, LANES), 0)
    lane8 = lane_index((8, LANES))
    wide = lane_index((1, WIDE))
    x_of = (wide // 8) % 4
    y_of = 2 * (wide % 4) + (wide // 4) % 2
    row_at = 2 * lax.broadcasted_iota(jnp.int32, (2, 8, WIDE), 1) + lax.broadcasted_iota(jnp.int32, (2, 8, WIDE), 0)
    row_weight = row_at.astype(jnp.float32)
    row_mask = jnp.where((row_at >= y_of) & (row_at <= y_of + 2 * REACH), 1.0, 0.0)
    pick = channels * ((lane8 // 8) % 4) + 8 * (lane8 % 4) + 4 * (sub8 % 2) + sub8 // 2
    beyond = [jnp.where(x_of > m, 9.0, 0.0) for m in range(3)]
    patch = [jnp.where(slot == q, 1.0, 0.0).astype(jnp.bfloat16) for q in range(per)]

    def gather(values, index):
        return jnp.take_along_axis(values, index, axis=1, mode="promise_in_bounds")

    starts = [0]
    for k in range(1, sections + 1):
        starts.append(starts[-1] + pl.cdiv(rows + 2 * REACH * (sections - k), 16))
    blocks = starts[-1]

    def place(t):
        t = jnp.clip(t, 0, blocks - 1)
        k, first = 1, 0
        for n in range(1, sections):
            k = k + jnp.where(t >= starts[n], 1, 0)
            first = jnp.where(t >= starts[n], starts[n], first)
        return k, 2 * (t - first)

    def scores(k, i, side):
        lhs, rhs = [], [[], []]
        for half in range(2):
            window = t_ref[k - 1, :, :, side, half, pl.ds(PAD + 1 + 4 * i, 8), :]
            lhs.append(window.reshape(16 * 16, LANES).astype(jnp.bfloat16))
            even = t_ref[k, 4:12, 0, side, half, pl.ds(PAD + 1 + 4 * i, 8), :]
            odd = t_ref[k, 4:12, 1, side, half, pl.ds(PAD - 3 + 4 * i, 8), :]
            current = jnp.where(sub8 < 4, even, odd) * scale
            current = current.reshape(64, LANES).astype(jnp.bfloat16)
            for h in range(2):
                mine = current[32 * h : 32 * (h + 1)]
                nothing = jnp.zeros_like(mine)
                for q in range(per):
                    masked = mine * patch[q]
                    rhs[h].append(jnp.concatenate([masked, nothing] if half == 0 else [nothing, masked], axis=1))
        lhs = jnp.concatenate(lhs, axis=1)
        return [
            lax.dot_general(
                lhs[64 * h : 64 * h + 192], jnp.concatenate(rhs[h], axis=0), (((1,), (1,)), ((), ())),
                preferred_element_type=jnp.float32,
            )
            for h in range(2)
        ]

    def means(source, at):
        for m in range(8, -1, -1):
            score = source[at, 16 * m : 16 * m + 16, :]
            if m < 3:
                score = jnp.where(x_of <= m, score, source[at, 16 * m + 144 : 16 * m + 160, :])
            term = jnp.exp2(score).reshape(2, 8, WIDE)
            running = running + term if m < 8 else term
            if m:
                moment = moment + running if m < 8 else running
            if m < 3:
                moment = moment + term * beyond[m]
        running = running * row_mask
        moment = moment * row_mask
        total = jnp.sum(running[0] + running[1], axis=0, keepdims=True)
        moved = running * row_weight
        y_sum = jnp.sum(moved[0] + moved[1], axis=0, keepdims=True)
        x_sum = jnp.sum(moment[0] + moment[1], axis=0, keepdims=True)
        return y_sum / total, x_sum / total

    def compose(k, i, down, across):
        extra = REACH * (sections - k)
        whole = jnp.floor(across)
        part = across - whole
        left = lane8 + whole.astype(jnp.int32)
        right = left + 1
        left_weight = jnp.where((left >= 0) & (left < LANES), 1.0 - part, 0.0)
        right_weight = jnp.where((right >= 0) & (right < LANES), part, 0.0)
        left = jnp.clip(left, 0, LANES - 1)
        right = jnp.clip(right, 0, LANES - 1)
        sums = [down, across]
        shift = jnp.where(k == 1, FIELD_HALO - REACH * sections, 0)
        for step in range(-REACH, REACH + 1):
            row_part = jnp.maximum(0.0, 1.0 - jnp.abs(down - step))
            for c in range(2):
                values = f_ref[k - 1, c, pl.ds(8 * i + REACH + step + shift, 8), :]
                mixed = left_weight * gather(values, left) + right_weight * gather(values, right)
                sums[c] = sums[c] + row_part * mixed
        row = sub8 + 8 * i - extra + tile * rows
        inside = (row >= 0) & (row < total_rows)
        return [jnp.where(inside, value, 0.0) for value in sums]

    def fill(t, target, n, side):
        k, i = place(t)
        target[4 * n + 2 * side], target[4 * n + 2 * side + 1] = scores(k, i + n, side)

    def finish(t, found):
        k, i = place(t)
        fields = [compose(k, i + n, found[2 * n], found[2 * n + 1]) for n in range(2)]
        for n in range(2):
            for c in range(2):
                f_ref[k, c, pl.ds(pl.multiple_of(8 * i + 8 * n, 8), 8), :] = fields[n][c]

    def step(t, carry, source, target):
        found = []
        for n in range(2):
            down = jnp.zeros((8, LANES), jnp.float32)
            across = jnp.zeros((8, LANES), jnp.float32)
            for side in range(2):
                fill(t + 1, target, n, side)
                for h in range(2):
                    at = 4 * n + 2 * side + h
                    y_mean, x_mean = means(source, at)
                    for half in range(2):
                        keep = (lane8 // 64 == side) & ((lane8 // 32) % 2 == half) & ((lane8 // 4) % 2 == h)
                        cols = slice(LANES * half, LANES * (half + 1))
                        down = jnp.where(keep, gather(jnp.broadcast_to(y_mean[:, cols], (8, LANES)), pick), down)
                        across = jnp.where(keep, gather(jnp.broadcast_to(x_mean[:, cols], (8, LANES)), pick), across)
            found.append(down - (REACH + sub8).astype(jnp.float32))
            found.append(across - (REACH + lane8 % 4).astype(jnp.float32))
        finish(t - 1, carry)
        return tuple(found)

    def two_steps(j, carry):
        carry = step(2 * j, carry, s0_ref, s1_ref)
        return step(2 * j + 1, carry, s1_ref, s0_ref)

    for at in range(4):
        fill(0, s0_ref, at // 2, at % 2)
    turns = pl.cdiv(blocks, 2)
    found = lax.fori_loop(0, turns, two_steps, (jnp.zeros((8, LANES), jnp.float32),) * 4)
    finish(2 * turns - 1, found)
    for k in range(1, sections + 1):
        extra = REACH * (sections - k)
        out_ref[k - 1] = f_ref[k, :, extra : extra + rows, :]


def on_device(images, section_order, prev_field, conv1_weight, conv1_bias, conv2_weight, conv2_bias):
    count = lax.axis_size("tile")
    forward = [(i, i + 1) for i in range(count - 1)]
    backward = [(target, source) for source, target in forward]
    pixel_rows, columns = images.shape[1:]
    sections = section_order.shape[0]
    rows = prev_field.shape[1]
    channels = conv1_weight.shape[0]

    vmem = pl.BlockSpec(memory_space=pltpu.VMEM)
    hbm = pl.BlockSpec(memory_space=pl.ANY)
    held = HALO + LATER * sections + FIELD_HALO
    up, down = pl.pallas_call(
        pack,
        out_shape=(jax.ShapeDtypeStruct((held, columns), images.dtype),) * 2,
        in_specs=[hbm, hbm],
        out_specs=(vmem, vmem),
        scratch_shapes=[
            pltpu.VMEM((2, 2, FIELD_HALO, prev_field.shape[2]), jnp.float32),
            pltpu.SemaphoreType.DMA((2, sections + 2)),
        ],
        compiler_params=pltpu.CompilerParams(vmem_limit_bytes=66850000),
        name="pack",
    )(images, prev_field)
    chain = section_order + 1
    lo = lax.ppermute(up, "tile", forward)
    hi = lax.ppermute(down, "tile", backward)

    w1, w2, b2 = pl.pallas_call(
        prepare,
        out_shape=(
            jax.ShapeDtypeStruct((WINDOWS, WIDE, WIDE), jnp.bfloat16),
            jax.ShapeDtypeStruct((LANES // channels, WIDE, WIDE), jnp.bfloat16),
            jax.ShapeDtypeStruct((8, LANES), jnp.float32),
        ),
        in_specs=[pl.BlockSpec(memory_space=pltpu.SMEM)] + [vmem] * 5,
        out_specs=(vmem,) * 3,
        cost_estimate=pl.CostEstimate(flops=10**9, bytes_accessed=10**6, transcendentals=0),
        compiler_params=pltpu.CompilerParams(vmem_limit_bytes=12 * 1024 * 1024),
        name="weights",
    )(chain, jnp.asarray(first_layer_lanes()), conv1_weight, conv1_bias[None], conv2_weight, conv2_bias[None])

    groups = columns // (4 * WINDOWS)
    span = (rows + 2 * REACH * sections) // 2 + 4
    return pl.pallas_call(
        functools.partial(kernel, sections, rows, rows * count, channels),
        out_shape=jax.ShapeDtypeStruct((sections, 2, rows, prev_field.shape[2]), jnp.float32),
        in_specs=[pl.BlockSpec(memory_space=pltpu.SMEM)] + [vmem] * 7,
        out_specs=vmem,
        scratch_shapes=[
            pltpu.VMEM((2, 2 * rows + 96, LANES), jnp.float32),
            pltpu.VMEM((groups * span, WIDE), jnp.bfloat16),
            pltpu.VMEM((2, groups, span + 2 * PAD, LANES), jnp.float32),
            pltpu.VMEM((2, groups, span + 2 * PAD, LANES), jnp.float32),
            pltpu.VMEM((2, groups, span, LANES), jnp.float32),
            pltpu.VMEM((2, groups, span, LANES), jnp.float32),
            pltpu.VMEM((sections + 1, 16, 2, 2, 2, span + 2 * PAD, LANES), jnp.float32),
            pltpu.VMEM((sections + 1, 2, rows + 2 * FIELD_HALO + 8, LANES), jnp.float32),
            pltpu.VMEM((8, 192, WIDE), jnp.float32),
            pltpu.VMEM((8, 192, WIDE), jnp.float32),
        ],
        compiler_params=pltpu.CompilerParams(vmem_limit_bytes=44 * 1024 * 1024),
        name="align",
    )(chain, images, lo, hi, prev_field, w1, w2, b2)


def solution(mesh):
    in_specs = (P("parts", "tile", None), P("parts"), P("parts", "tile", None), P(), P(), P(), P())
    out_specs = P("parts", None, "tile", None)
    return jax.shard_map(on_device, mesh=mesh, in_specs=in_specs, out_specs=out_specs, check_vma=False)
```

```python
import functools
import math

import jax
import jax.numpy as jnp
import numpy as np
from jax import lax
from jax.experimental import pallas as pl
from jax.experimental.pallas import tpu as pltpu
from jax.sharding import PartitionSpec as P

SHARPNESS = 16.0
REACH = 4
LANES = 128
WIDE = 256
HALO = 32
LATER = 24
FIELD_HALO = 16
PITCH = 40
BIAS_LANE = 248
PAD = 8
WINDOWS = 8


def first_layer_lanes():
    lanes = np.full((1, LANES), -WIDE, np.int32)
    for slot in range(8):
        for tap in range(9):
            pixel_row = 2 * (slot // 4) + tap // 3
            start = PITCH * pixel_row if pixel_row < 3 else LANES + PITCH * (pixel_row - 3)
            lanes[0, 9 * slot + tap] = start + 2 * (slot % 4) + tap % 3
    return lanes


def pack(img_ref, fld_ref, up_ref, down_ref, field_ref, sem):
    sections = img_ref.shape[0] - 1
    copies = []
    for side, out_ref in enumerate((up_ref, down_ref)):
        at = 0
        for section in range(sections + 1):
            count = LATER if section else HALO
            first = 0 if side else img_ref.shape[1] - count
            copies.append(
                pltpu.make_async_copy(
                    img_ref.at[section, first : first + count], out_ref.at[at : at + count], sem.at[side, section]
                )
            )
            at += count
        first = 0 if side else fld_ref.shape[1] - FIELD_HALO
        copies.append(
            pltpu.make_async_copy(
                fld_ref.at[:, first : first + FIELD_HALO], field_ref.at[side], sem.at[side, sections + 1]
            )
        )
    for copy in copies:
        copy.start()
    for copy in copies:
        copy.wait()
    for side, out_ref in enumerate((up_ref, down_ref)):
        field = jnp.concatenate([field_ref[side, 0], field_ref[side, 1]], axis=1)
        out_ref[HALO + LATER * sections :, :] = field.astype(jnp.bfloat16)


def prepare(chain_ref, lanes_ref, c1_ref, b1_ref, c2_ref, b2_ref, w1_ref, w2_ref, bias_ref):
    del chain_ref
    channels, taps = c1_ref.shape

    def indices(shape):
        return [lax.broadcasted_iota(jnp.int32, shape, axis) for axis in range(2)]

    def ones_where(condition):
        return jnp.where(condition, 1.0, 0.0).astype(jnp.bfloat16)

    def repeated(values, dims):
        return lax.dot_general(values, spread, (dims, ((), ())), preferred_element_type=jnp.float32)

    row, col = indices((channels, WIDE))
    spread = ones_where(col % channels == row)

    def pieces(ref):
        rest = jnp.broadcast_to(ref[...], (8, channels))
        row = lax.broadcasted_iota(jnp.int32, (8, channels), 0)
        total = jnp.zeros((8, channels), jnp.float32)
        for n in range(3):
            top = rest.astype(jnp.bfloat16).astype(jnp.float32)
            total = jnp.where(row == n, top, total)
            rest = rest - top
        return repeated(total.astype(jnp.bfloat16), ((1,), (0,)))

    bias_ref[...] = jnp.broadcast_to(jnp.sum(pieces(b2_ref), axis=0, keepdims=True), (8, WIDE))[:, :LANES]

    by_tap = repeated(c1_ref[...], ((0,), (0,)))
    row, col = indices((LANES, WIDE))
    table = jnp.zeros((LANES, WIDE), jnp.float32)
    slot = col // channels
    for tap in range(taps):
        table = jnp.where(row == taps * slot + tap, by_tap[tap : tap + 1], table)
    bias = pieces(b1_ref)
    for n in range(3):
        table = jnp.where(row == 8 * taps + n, bias[n : n + 1], table)
    table = table.astype(jnp.bfloat16)
    row, col = indices((WIDE, LANES))
    bias_lane = (col >= 8 * taps) & (col < 8 * taps + 3) & (row == BIAS_LANE + col - 8 * taps)
    for window in range(WINDOWS):
        pick = ones_where((row == lanes_ref[...] + 4 * window) | bias_lane)
        w1_ref[window] = jnp.dot(pick, table, preferred_element_type=jnp.float32).astype(jnp.bfloat16)

    row, col = indices((WIDE, WIDE))
    slot_in, slot_out = row // channels, col // channels
    row_out = slot_out // 2
    row_out = jnp.where(row_out == 0, 2, row_out - 2)
    row_step = slot_in // 4 - row_out
    col_step = slot_in % 4 - 1 - slot_out % 2
    near = (jnp.abs(row_step) <= 1) & (jnp.abs(col_step) <= 1)
    tap_at = jnp.where(near, 3 * row_step + col_step + 4, -1)
    table = jnp.zeros((WIDE, WIDE), jnp.float32)
    for tap in range(taps):
        block = repeated(c2_ref[tap], ((0,), (0,)))
        table = jnp.where(tap_at == tap, jnp.concatenate([block] * (WIDE // channels), axis=0), table)
    table = table.astype(jnp.bfloat16)
    for skew in range(LANES // channels):
        for half in range(2):
            cols = slice(LANES * half, LANES * (half + 1))
            part = table[:, cols]
            w2_ref[skew, :, cols] = pltpu.roll(part, channels * skew, 1) if skew else part


def lane_index(shape):
    return lax.broadcasted_iota(jnp.int32, shape, len(shape) - 1)


def kernel(
    sections, rows, total_rows, channels,
    chain_ref, img_ref, lo_ref, hi_ref, fld_ref, w1_ref, w2_ref, b2_ref,
    out_ref, z_ref, x_ref, a0_ref, a1_ref, b0_ref, b1_ref, t_ref, f_ref, s0_ref, s1_ref,
):
    groups = a0_ref.shape[1]
    largest = x_ref.shape[0] // groups
    per = LANES // channels
    lane = lane_index((1, LANES))
    slot = lane // channels
    tile = lax.axis_index("tile")
    pairs_total = total_rows // 2

    z_ref[...] = jnp.zeros_like(z_ref)
    pictures = HALO + LATER * sections
    f_ref[0, :, FIELD_HALO : FIELD_HALO + rows, :] = fld_ref[...]
    for ref, start in ((lo_ref, 0), (hi_ref, FIELD_HALO + rows)):
        for c in range(2):
            part = ref[pictures : pictures + FIELD_HALO, LANES * c : LANES * (c + 1)]
            f_ref[0, c, start : start + FIELD_HALO, :] = part.astype(jnp.float32)

    def inside_mask(k, span):
        pair = lax.broadcasted_iota(jnp.int32, (span, LANES), 0) + tile * (rows // 2) - 1
        pair = pair - REACH * (sections - k) // 2
        return jnp.where((pair >= 0) & (pair < pairs_total), 1.0, 0.0)

    def layers(xh, target, span):
        for part in range(2):
            first = jnp.dot(x_ref[: groups * span], w1_ref[xh + 4 * part], preferred_element_type=jnp.float32)
            first = jnp.maximum(first, 0.0)
            edge = (lane_index((1, WIDE)) // channels) % 4
            if xh == 0 and part == 0:
                first = jnp.concatenate([jnp.where(edge == 0, 0.0, first[:span]), first[span:]], axis=0)
            if xh == 3 and part == 1:
                first = jnp.concatenate([first[:-span], jnp.where(edge == 3, 0.0, first[-span:])], axis=0)
            first = first.astype(jnp.bfloat16)
            for odd in range(2):
                half = groups * span // 2
                second = jnp.dot(
                    first[half * odd : half * (odd + 1)], w2_ref[part + 2 * odd], preferred_element_type=jnp.float32
                )
                at = groups // 2 * odd
                second = second.reshape(groups // 2, span, WIDE)
                target[0][part, at : at + groups // 2, PAD : PAD + span, :] = second[:, :, :LANES]
                target[1][part, at : at + groups // 2, 0:span, :] = second[:, :, LANES:]

    def features(k, xh, source, span):
        valid = inside_mask(k, span)
        for side in range(2):
            for half in range(2):
                parts = []
                for q in range(per):
                    part, odd = q % 2, q // 2
                    at = 2 * side + half + 4 * odd
                    above = source[0][part, at, PAD - 1 : PAD - 1 + span, :]
                    below = source[0][part, at, PAD + 1 : PAD + 1 + span, :]
                    here = source[1][part, at, 0:span, :]
                    summed = here + jnp.where((slot + per - q) % per < 2, above, below)
                    parts.append(jnp.tanh(summed + b2_ref[0:1, :]) * valid)
                for t in range(per):
                    value = parts[0]
                    for q in range(1, per):
                        value = jnp.where(slot == (t + q) % per, parts[q], value)

                    def turned(by):
                        by = channels * (by - t) % LANES
                        return pltpu.roll(value, by, 1) if by else value

                    parity, pixel = t // 2, t % 2
                    column = 2 * xh + pixel
                    lines = slice(PAD, PAD + span)
                    t_ref[k, 4 + column, parity, side, half, lines, :] = turned(0)
                    if isinstance(k, int) and k == sections:
                        continue
                    n = 2 * side + half
                    step, edge, border = (1, 0, column - 4) if xh >= 2 else (-1, per - 1, 12 + column)
                    moved = turned(step)
                    own = t_ref.at[k, border, parity, side, half, lines, :]
                    if 0 <= n + step < 4:
                        other = t_ref.at[k, border, parity, (n + step) // 2, (n + step) % 2, lines, :]
                        pltpu.store(other, moved, mask=jnp.broadcast_to(slot == edge, moved.shape))
                    if 0 <= n - step < 4:
                        pltpu.store(own, moved, mask=jnp.broadcast_to(slot != edge, moved.shape))
                    else:
                        own[...] = jnp.where(slot == edge, 0.0, moved)

    def encode(span, before, k, carry):
        extra = REACH * (sections - k)
        section = jnp.where(k == 0, 0, chain_ref[jnp.maximum(k - 1, 0)])
        first = jnp.where(k == 0, 0, HALO + LATER * (section - 1))
        low = pl.ds(pl.multiple_of(first + jnp.where(k == 0, HALO - LATER, 0), 8), LATER)
        high = pl.ds(pl.multiple_of(first, 8), LATER)
        base = pl.multiple_of(2 * extra + HALO, 8)
        for half in range(2):
            cols = slice(LANES * half, LANES * (half + 1))
            z_ref[half, pl.ds(base - LATER, LATER), :] = lo_ref[low, cols].astype(jnp.float32)
            z_ref[half, pl.ds(base, 2 * rows), :] = img_ref[section, :, cols].astype(jnp.float32)
            z_ref[half, pl.ds(base + 2 * rows, LATER), :] = hi_ref[high, cols].astype(jnp.float32)

        @pl.when(k == 0)
        def _():
            for half in range(2):
                cols = slice(LANES * half, LANES * (half + 1))
                far = HALO - LATER
                z_ref[half, pl.ds(base - HALO, far), :] = lo_ref[0:far, cols].astype(jnp.float32)
                z_ref[half, pl.ds(base + 2 * rows + LATER, far), :] = hi_ref[LATER:HALO, cols].astype(jnp.float32)

        valid = inside_mask(k, span)
        for group in range(groups):
            side, place = divmod(group, groups // 2)
            at = group // 2 + groups // 2 * (group % 2)
            pieces = []
            for row in range(5):
                here = z_ref[side, pl.ds(HALO - 5 + row, span, stride=4), :]
                if place == 0 or (place == groups // 2 - 1 and side == 0):
                    if side == 0 and place == 0:
                        here = jnp.where(lane < LANES // 2, here, 0.0)
                    else:
                        other = z_ref[1 - side, pl.ds(HALO - 5 + row, span, stride=4), :]
                        low, high = (here, other) if side == 1 else (other, here)
                        here = jnp.where(lane < LANES // 2, low, high)
                start = PITCH * (row % 3)
                shift = (start - (2 * LANES // groups * place - 3)) % LANES
                pieces.append(pltpu.roll(here.astype(jnp.bfloat16), shift, 1))
            left = jnp.where(lane < PITCH, pieces[0], jnp.where(lane < 2 * PITCH, pieces[1], pieces[2]))
            right = jnp.where(lane < PITCH, pieces[3], jnp.where(lane < BIAS_LANE - LANES, pieces[4], valid.astype(jnp.bfloat16)))
            x_ref[pl.ds(span * at, span), 0:LANES] = left * valid.astype(jnp.bfloat16)
            x_ref[pl.ds(span * at, span), LANES:WIDE] = right * valid.astype(jnp.bfloat16)

        buffers = ((a0_ref, b0_ref), (a1_ref, b1_ref))
        for xh in range(4):
            layers(xh, buffers[xh % 2], span)
            last = buffers[(xh - 1) % 2]
            if xh:
                features(k, xh - 1, last, span)
            else:
                features(jnp.maximum(k - 1, 0), 3, last, before)
        return carry

    half = (sections + 1) // 2
    fewer = pl.cdiv((rows + 2 * REACH * (sections - half)) // 2 + 2, 8) * 8
    lax.fori_loop(0, half, functools.partial(encode, largest, largest), 0)
    encode(fewer, largest, half, 0)
    lax.fori_loop(half + 1, sections + 1, functools.partial(encode, fewer, fewer), 0)

    scale = SHARPNESS / channels * math.log2(math.e)
    sub8 = lax.broadcasted_iota(jnp.int32, (8, LANES), 0)
    lane8 = lane_index((8, LANES))
    wide = lane_index((1, WIDE))
    x_of = (wide // 8) % 4
    y_of = 2 * (wide % 4) + (wide // 4) % 2
    row_at = 2 * lax.broadcasted_iota(jnp.int32, (2, 8, WIDE), 1) + lax.broadcasted_iota(jnp.int32, (2, 8, WIDE), 0)
    row_weight = row_at.astype(jnp.float32)
    row_mask = jnp.where((row_at >= y_of) & (row_at <= y_of + 2 * REACH), 1.0, 0.0)
    pick = channels * ((lane8 // 8) % 4) + 8 * (lane8 % 4) + 4 * (sub8 % 2) + sub8 // 2
    beyond = [jnp.where(x_of > m, 9.0, 0.0) for m in range(3)]
    patch = [jnp.where(slot == q, 1.0, 0.0).astype(jnp.bfloat16) for q in range(per)]

    def gather(values, index):
        return jnp.take_along_axis(values, index, axis=1, mode="promise_in_bounds")

    starts = [0]
    for k in range(1, sections + 1):
        starts.append(starts[-1] + pl.cdiv(rows + 2 * REACH * (sections - k), 16))
    blocks = starts[-1]

    def place(t):
        t = jnp.clip(t, 0, blocks - 1)
        k, first = 1, 0
        for n in range(1, sections):
            k = k + jnp.where(t >= starts[n], 1, 0)
            first = jnp.where(t >= starts[n], starts[n], first)
        return k, 2 * (t - first)

    def scores(k, i, side):
        lhs, rhs = [], [[], []]
        for half in range(2):
            window = t_ref[k - 1, :, :, side, half, pl.ds(PAD + 1 + 4 * i, 8), :]
            lhs.append(window.reshape(16 * 16, LANES).astype(jnp.bfloat16))
            even = t_ref[k, 4:12, 0, side, half, pl.ds(PAD + 1 + 4 * i, 8), :]
            odd = t_ref[k, 4:12, 1, side, half, pl.ds(PAD - 3 + 4 * i, 8), :]
            current = jnp.where(sub8 < 4, even, odd) * scale
            current = current.reshape(64, LANES).astype(jnp.bfloat16)
            for h in range(2):
                mine = current[32 * h : 32 * (h + 1)]
                nothing = jnp.zeros_like(mine)
                for q in range(per):
                    masked = mine * patch[q]
                    rhs[h].append(jnp.concatenate([masked, nothing] if half == 0 else [nothing, masked], axis=1))
        lhs = jnp.concatenate(lhs, axis=1)
        return [
            lax.dot_general(
                lhs[64 * h : 64 * h + 192], jnp.concatenate(rhs[h], axis=0), (((1,), (1,)), ((), ())),
                preferred_element_type=jnp.float32,
            )
            for h in range(2)
        ]

    def means(source, at):
        for m in range(8, -1, -1):
            score = source[at, 16 * m : 16 * m + 16, :]
            if m < 3:
                score = jnp.where(x_of <= m, score, source[at, 16 * m + 144 : 16 * m + 160, :])
            term = jnp.exp2(score).reshape(2, 8, WIDE)
            running = running + term if m < 8 else term
            if m:
                moment = moment + running if m < 8 else running
            if m < 3:
                moment = moment + term * beyond[m]
        running = running * row_mask
        moment = moment * row_mask
        total = jnp.sum(running[0] + running[1], axis=0, keepdims=True)
        moved = running * row_weight
        y_sum = jnp.sum(moved[0] + moved[1], axis=0, keepdims=True)
        x_sum = jnp.sum(moment[0] + moment[1], axis=0, keepdims=True)
        return y_sum / total, x_sum / total

    def compose(k, i, down, across):
        extra = REACH * (sections - k)
        whole = jnp.floor(across)
        part = across - whole
        left = lane8 + whole.astype(jnp.int32)
        right = left + 1
        left_weight = jnp.where((left >= 0) & (left < LANES), 1.0 - part, 0.0)
        right_weight = jnp.where((right >= 0) & (right < LANES), part, 0.0)
        left = jnp.clip(left, 0, LANES - 1)
        right = jnp.clip(right, 0, LANES - 1)
        sums = [down, across]
        shift = jnp.where(k == 1, FIELD_HALO - REACH * sections, 0)
        for step in range(-REACH, REACH + 1):
            row_part = jnp.maximum(0.0, 1.0 - jnp.abs(down - step))
            for c in range(2):
                values = f_ref[k - 1, c, pl.ds(8 * i + REACH + step + shift, 8), :]
                mixed = left_weight * gather(values, left) + right_weight * gather(values, right)
                sums[c] = sums[c] + row_part * mixed
        row = sub8 + 8 * i - extra + tile * rows
        inside = (row >= 0) & (row < total_rows)
        return [jnp.where(inside, value, 0.0) for value in sums]

    def fill(t, target, n, side):
        k, i = place(t)
        target[4 * n + 2 * side], target[4 * n + 2 * side + 1] = scores(k, i + n, side)

    def finish(t, found):
        k, i = place(t)
        fields = [compose(k, i + n, found[2 * n], found[2 * n + 1]) for n in range(2)]
        for n in range(2):
            for c in range(2):
                f_ref[k, c, pl.ds(pl.multiple_of(8 * i + 8 * n, 8), 8), :] = fields[n][c]

    def step(t, carry, source, target):
        found = []
        for n in range(2):
            down = jnp.zeros((8, LANES), jnp.float32)
            across = jnp.zeros((8, LANES), jnp.float32)
            for side in range(2):
                fill(t + 1, target, n, side)
                for h in range(2):
                    at = 4 * n + 2 * side + h
                    y_mean, x_mean = means(source, at)
                    for half in range(2):
                        keep = (lane8 // 64 == side) & ((lane8 // 32) % 2 == half) & ((lane8 // 4) % 2 == h)
                        cols = slice(LANES * half, LANES * (half + 1))
                        down = jnp.where(keep, gather(jnp.broadcast_to(y_mean[:, cols], (8, LANES)), pick), down)
                        across = jnp.where(keep, gather(jnp.broadcast_to(x_mean[:, cols], (8, LANES)), pick), across)
            found.append(down - (REACH + sub8).astype(jnp.float32))
            found.append(across - (REACH + lane8 % 4).astype(jnp.float32))
        finish(t - 1, carry)
        return tuple(found)

    def two_steps(j, carry):
        carry = step(2 * j, carry, s0_ref, s1_ref)
        return step(2 * j + 1, carry, s1_ref, s0_ref)

    for at in range(4):
        fill(0, s0_ref, at // 2, at % 2)
    features(sections, 3, (a1_ref, b1_ref), fewer)
    turns = pl.cdiv(blocks, 2)
    found = lax.fori_loop(0, turns, two_steps, (jnp.zeros((8, LANES), jnp.float32),) * 4)
    finish(2 * turns - 1, found)
    for k in range(1, sections + 1):
        extra = REACH * (sections - k)
        out_ref[k - 1] = f_ref[k, :, extra : extra + rows, :]


def on_device(images, section_order, prev_field, conv1_weight, conv1_bias, conv2_weight, conv2_bias):
    count = lax.axis_size("tile")
    forward = [(i, i + 1) for i in range(count - 1)]
    backward = [(target, source) for source, target in forward]
    pixel_rows, columns = images.shape[1:]
    sections = section_order.shape[0]
    rows = prev_field.shape[1]
    channels = conv1_weight.shape[0]

    vmem = pl.BlockSpec(memory_space=pltpu.VMEM)
    hbm = pl.BlockSpec(memory_space=pl.ANY)
    held = HALO + LATER * sections + FIELD_HALO
    up, down = pl.pallas_call(
        pack,
        out_shape=(jax.ShapeDtypeStruct((held, columns), images.dtype),) * 2,
        in_specs=[hbm, hbm],
        out_specs=(vmem, vmem),
        scratch_shapes=[
            pltpu.VMEM((2, 2, FIELD_HALO, prev_field.shape[2]), jnp.float32),
            pltpu.SemaphoreType.DMA((2, sections + 2)),
        ],
        compiler_params=pltpu.CompilerParams(vmem_limit_bytes=66850000),
        name="pack",
    )(images, prev_field)
    chain = section_order + 1
    lo = lax.ppermute(up, "tile", forward)
    hi = lax.ppermute(down, "tile", backward)

    w1, w2, b2 = pl.pallas_call(
        prepare,
        out_shape=(
            jax.ShapeDtypeStruct((WINDOWS, WIDE, WIDE), jnp.bfloat16),
            jax.ShapeDtypeStruct((LANES // channels, WIDE, WIDE), jnp.bfloat16),
            jax.ShapeDtypeStruct((8, LANES), jnp.float32),
        ),
        in_specs=[pl.BlockSpec(memory_space=pltpu.SMEM)] + [vmem] * 5,
        out_specs=(vmem,) * 3,
        cost_estimate=pl.CostEstimate(flops=10**9, bytes_accessed=10**6, transcendentals=0),
        compiler_params=pltpu.CompilerParams(vmem_limit_bytes=12 * 1024 * 1024),
        name="weights",
    )(chain, jnp.asarray(first_layer_lanes()), conv1_weight, conv1_bias[None], conv2_weight, conv2_bias[None])

    groups = columns // (4 * WINDOWS)
    span = (rows + 2 * REACH * sections) // 2 + 4
    return pl.pallas_call(
        functools.partial(kernel, sections, rows, rows * count, channels),
        out_shape=jax.ShapeDtypeStruct((sections, 2, rows, prev_field.shape[2]), jnp.float32),
        in_specs=[pl.BlockSpec(memory_space=pltpu.SMEM)] + [vmem] * 7,
        out_specs=vmem,
        scratch_shapes=[
            pltpu.VMEM((2, 2 * rows + 96, LANES), jnp.float32),
            pltpu.VMEM((groups * span, WIDE), jnp.bfloat16),
            pltpu.VMEM((2, groups, span + 2 * PAD, LANES), jnp.float32),
            pltpu.VMEM((2, groups, span + 2 * PAD, LANES), jnp.float32),
            pltpu.VMEM((2, groups, span, LANES), jnp.float32),
            pltpu.VMEM((2, groups, span, LANES), jnp.float32),
            pltpu.VMEM((sections + 1, 16, 2, 2, 2, span + 2 * PAD, LANES), jnp.float32),
            pltpu.VMEM((sections + 1, 2, rows + 2 * FIELD_HALO + 8, LANES), jnp.float32),
            pltpu.VMEM((8, 192, WIDE), jnp.float32),
            pltpu.VMEM((8, 192, WIDE), jnp.float32),
        ],
        compiler_params=pltpu.CompilerParams(vmem_limit_bytes=44 * 1024 * 1024),
        name="align",
    )(chain, images, lo, hi, prev_field, w1, w2, b2)


def solution(mesh):
    in_specs = (P("parts", "tile", None), P("parts"), P("parts", "tile", None), P(), P(), P(), P())
    out_specs = P("parts", None, "tile", None)
    return jax.shard_map(on_device, mesh=mesh, in_specs=in_specs, out_specs=out_specs, check_vma=False)
```
